128 devices in a mesh: chan: 16 (over z, x_hi, core), seg: 8 (over y, x_lo).
Axes of the slice: x: 4 (x_hi: 2, x_lo: 2; x = x_hi * 2 + x_lo), y: 4, z: 4, core: 2. Of those that a mesh axis runs over, the one named last changes fastest.
Arguments:
- traces: float32 [32, 128, 7680], P('seg', None, 'chan'), may hold values from -40 to 40
- sources: int32 [64], replicated, may hold values from 0 to 127, as said below
- validity: int32 [32, 128], replicated, may hold values from 0 to 1, as said below
Outputs:
- correlation: float32 [64, 128, 512], P('seg', 'chan')
The draws below stay inside these ranges and needn't reach their ends.
Inputs may be any that keep to these rules, and one draw needn't show every extreme that they name: `sources`: 64 distinct channel indices. `validity`: 1 marks a usable segment of a channel, 0 a discarded one; in every draw some channels are 0 in all segments.
All inputs are finite; a program needn't handle non-finite values.
Results may differ from the reference program's by a relative error of at most 0.0021.
Values may be sent and summed in bfloat16 or wider, within the bound.
A program may use at most 128 MiB of HBM per device.

```python
import math
import jax
import jax.numpy as jnp
from jax import lax

L = 7680
NF = 3840
LAGS = 512
SRC = 64
CH = 128
SEG = 32


def draw_traces(key, part):
    noise_key, scale_key, tap_key, wave_key = jax.random.split(key, 4)
    noise_draw = jnp.clip(jax.random.normal(noise_key, (SEG, CH, L + 1), jnp.float32), -4.5, 4.5)
    scales = jnp.exp(jax.random.uniform(scale_key, (SEG, CH, 1), jnp.float32, math.log(0.3), math.log(3.0)))
    strength = 0.03
    tap_weight = jax.random.uniform(tap_key, (SEG, CH, 1), jnp.float32, -0.8, 0.8)
    colored = noise_draw[:, :, 1:] + tap_weight * noise_draw[:, :, :-1]
    common_wave = jnp.clip(jax.random.normal(wave_key, (SEG, L), jnp.float32), -4.5, 4.5)
    positions = (jnp.arange(L, dtype=jnp.int32)[None, :] - 2 * jnp.arange(CH, dtype=jnp.int32)[:, None]) % L
    common = common_wave[:, positions]
    return scales * colored + strength * common


def draw_sources(key, part):
    inner_key, order_key = jax.random.split(key)
    middle = jax.random.permutation(inner_key, CH - 2)[:SRC - 2].astype(jnp.int32) + 1
    chosen = jnp.concatenate([jnp.array([0, CH - 1], dtype=jnp.int32), middle])
    return chosen[jax.random.permutation(order_key, SRC)]


def draw_validity(key, part):
    dead_key, pick_key, kept_key = jax.random.split(key, 3)
    dead_channel = jax.random.randint(dead_key, (CH,), 0, 12) == 0
    forced = jax.random.randint(pick_key, (), 0, CH)
    dead_channel = dead_channel | (jnp.arange(CH, dtype=jnp.int32) == forced)
    kept_cells = jax.random.randint(kept_key, (SEG, CH), 0, 4) != 0
    return (kept_cells & jnp.logical_not(dead_channel[None, :])).astype(jnp.int32)


def setup_inputs(seed: int = 0) -> dict:
    splits = jax.random.split(jax.random.key(seed), 4)
    return {
        "traces": draw_traces(jax.random.fold_in(splits[3], 71), 0),
        "sources": draw_sources(jax.random.fold_in(splits[3], 71), 0),
        "validity": draw_validity(jax.random.fold_in(splits[3], 71), 0),
    }


EPSILON = 1e-06

def whiten_all(traces):
    spectrum = jnp.fft.rfft(traces, axis=-1)[..., :NF]
    real_part = jnp.real(spectrum)
    imag_part = jnp.imag(spectrum)
    magnitude = jnp.sqrt(real_part * real_part + imag_part * imag_part)
    grouped = magnitude.reshape(magnitude.shape[:-1] + (NF // 128, 128))
    level = jnp.repeat(lax.optimization_barrier(jnp.mean(grouped, axis=-1)) + EPSILON, 128, axis=-1)
    return ((real_part / level).astype(jnp.bfloat16), (imag_part / level).astype(jnp.bfloat16))

def reference(traces, sources, validity):
    real_white, imag_white = whiten_all(traces)
    valid_cells = validity.astype(jnp.float32)
    valid_gate = valid_cells[:, :, None].astype(jnp.bfloat16)
    real_data = (real_white * valid_gate).astype(jnp.float32)
    imag_data = (imag_white * valid_gate).astype(jnp.float32)
    source_valid = jnp.take(valid_cells, sources, axis=1)
    pairs = jnp.dot(source_valid.T, valid_cells, precision=lax.Precision.HIGHEST, preferred_element_type=jnp.float32)
    half_lags = LAGS // 2

    def one_source(source_id):
        src_real = jnp.take(real_data, source_id, axis=1)[:, None, :]
        src_imag = jnp.take(imag_data, source_id, axis=1)[:, None, :]
        stack_real = lax.optimization_barrier(jnp.sum(src_real * real_data + src_imag * imag_data, axis=0))
        stack_imag = lax.optimization_barrier(jnp.sum(src_real * imag_data - src_imag * real_data, axis=0))
        spectrum_full = jnp.pad(lax.complex(stack_real, stack_imag), ((0, 0), (0, 1)))
        circular = jnp.fft.irfft(spectrum_full, n=L, axis=-1) * L
        return jnp.concatenate([circular[:, L - half_lags:], circular[:, :half_lags]], axis=1)
    correlation = lax.map(one_source, sources)
    return correlation / jnp.sqrt(2.0 * NF * jnp.maximum(pairs, 1.0))[:, :, None]
```

```python
import functools
import math

import jax
import jax.numpy as jnp
import numpy as np
from jax import lax
from jax.experimental import pallas as pl
from jax.experimental.pallas import tpu as pltpu
from jax.sharding import PartitionSpec as P

LAGS = 512
EPSILON = 1e-06
MESH = pl.DeviceIdType.MESH
CHUNKS = 4
F32 = jnp.float32
BF16 = jnp.bfloat16


def constant_tables(length, blocks):
    block_len = length // blocks
    half = block_len // 2
    q = np.arange(block_len)[:, None]
    k1 = np.arange(blocks)[:, None]
    k2 = np.arange(half)[None, :]
    angle = 2.0 * math.pi / length * ((k1 * q.T) % length)
    twist = np.zeros((2, blocks, 512), np.float32)
    twist[0, :, :block_len] = np.cos(angle)
    twist[1, :, :block_len] = np.sin(angle)
    angle = 2.0 * math.pi / block_len * ((q * k2) % block_len)
    second = np.zeros((2, 512, 256), np.float32)
    second[0, :block_len, :half] = np.cos(angle)
    second[1, :block_len, :half] = np.sin(angle)
    second_hi = second.astype(jnp.bfloat16)
    second_lo = (second - second_hi.astype(np.float32)).astype(jnp.bfloat16)
    lag = (np.arange(LAGS) - LAGS // 2)[None, :]
    angle = 2.0 * math.pi / length * ((k1 * lag) % length)
    lag_one = np.stack([np.cos(angle), np.sin(angle)]).astype(np.float32)
    angle = 2.0 * math.pi / block_len * ((k2.T * lag) % block_len)
    lag_two = np.zeros((2, 256, LAGS), np.float32)
    lag_two[0, :half] = 2.0 * np.cos(angle)
    lag_two[1, :half] = 2.0 * np.sin(angle)
    return twist, second_hi, second_lo, lag_one, lag_two


def times_root(value, k, n):
    re, im = value
    c, s = math.cos(2.0 * math.pi * k / n), math.sin(2.0 * math.pi * k / n)
    if k == 0:
        return value
    if 4 * k == n:
        return (im, -re)
    if 2 * k == n:
        return (-re, None if im is None else -im)
    if im is None:
        return (re * c, re * (-s))
    return (re * c + im * s, im * c - re * s)


def plus(a, b):
    if a is None:
        return b
    return a if b is None else a + b


def conj(value):
    re, im = value
    return (re, None if im is None else -im)


def real_dft(xs):
    n = len(xs)
    if n == 2:
        return [(xs[0] + xs[1], None), (xs[0] - xs[1], None)]
    even, odd = real_dft(xs[0::2]), real_dft(xs[1::2])
    h = n // 2
    out = []
    for k in range(h + 1):
        i = k % h
        e = even[i] if i <= h // 2 else conj(even[h - i])
        o = odd[i] if i <= h // 2 else conj(odd[h - i])
        t = times_root(o, k, n)
        out.append((plus(e[0], t[0]), plus(e[1], t[1])))
    return out


def split(value):
    hi = value.astype(BF16)
    return hi, (value - hi.astype(F32)).astype(BF16)


def dot(a, b):
    return jnp.dot(a, b, preferred_element_type=F32)


def body(
    sources,
    traces,
    validity,
    twist,
    second_hi,
    second_lo,
    lag_one,
    lag_two,
    out,
    src_send,
    own_recv,
    src_recv,
    h_hi,
    h_lo,
    table_hi,
    table_lo,
    spec,
    own_white,
    gathered,
    lag_table,
    prod,
    acc,
    part_recv,
    own_ss,
    own_rs,
    src_ss,
    src_rs,
    ag_ss,
    ag_rs,
    fw_ss,
    fw_rs,
    rs_ss,
    rs_rs,
):
    chans = lax.axis_size("chan")
    segs = lax.axis_size("seg")
    chips = chans // 2
    me = lax.axis_index("chan")
    seg = lax.axis_index("seg")
    chip = me // 2
    core = me % 2
    block_len = traces.shape[2]

    barrier = pltpu.get_barrier_semaphore()
    for d in range(1, chans):
        pl.semaphore_signal(
            barrier, inc=1, device_id=((me + d) % chans, seg), device_id_type=MESH
        )
    for d in range(1, segs):
        pl.semaphore_signal(
            barrier, inc=1, device_id=(me, (seg + d) % segs), device_id_type=MESH
        )

    def pick(s, carry):
        src_send[:, pl.ds(s, 1), :] = traces[:, pl.ds(sources[s], 1), :]
        return carry

    lax.fori_loop(0, 8 * chips, pick, 0)
    pl.semaphore_wait(barrier, chans - 1 + segs - 1)

    src_copies, own_copies = [], []
    for d in range(1, chans):
        to = (me + d) % chans
        copy = pltpu.make_async_remote_copy(
            src_ref=src_send.at[pl.ds(2 * (to % 2), 2), pl.ds(8 * (to // 2), 8)],
            dst_ref=src_recv.at[me],
            send_sem=src_ss.at[d],
            recv_sem=src_rs.at[d],
            device_id=(to, seg),
            device_id_type=MESH,
        )
        copy.start()
        src_copies.append(copy)
    for d in range(1, chans):
        to = (me + d) % chans
        copy = pltpu.make_async_remote_copy(
            src_ref=traces.at[:, pl.ds(8 * to, 8)],
            dst_ref=own_recv.at[me],
            send_sem=own_ss.at[d],
            recv_sem=own_rs.at[d],
            device_id=(to, seg),
            device_id_type=MESH,
        )
        copy.start()
        own_copies.append(copy)
    src_recv[pl.ds(me, 1)] = src_send[
        pl.ds(2 * core, 2), pl.ds(pl.multiple_of(8 * chip, 8), 8), :
    ][None]
    own_recv[pl.ds(me, 1)] = traces[:, pl.ds(pl.multiple_of(8 * me, 8), 8), :][None]

    table_hi[:512, :256] = second_hi[0]
    table_hi[512:, :256] = second_hi[1]
    table_hi[:512, 256:] = -second_hi[1]
    table_hi[512:, 256:] = second_hi[0]
    table_lo[:512, :256] = second_lo[0]
    table_lo[512:, :256] = second_lo[1]
    table_lo[:512, 256:] = -second_lo[1]
    table_lo[512:, 256:] = second_lo[0]

    def fill(k1, carry):
        c1 = lag_one[0, pl.ds(k1, 1), :]
        s1 = lag_one[1, pl.ds(k1, 1), :]

        def rows(i, inner):
            r = pl.multiple_of(i * 16, 16)
            c2 = lag_two[0, pl.ds(r, 16), :]
            s2 = lag_two[1, pl.ds(r, 16), :]
            lag_table[k1, pl.ds(r, 16), :] = (c1 * c2 - s1 * s2).astype(BF16)
            lag_table[k1, pl.ds(r + 256, 16), :] = (-(s1 * c2 + c1 * s2)).astype(BF16)
            return inner

        return lax.fori_loop(0, 16, rows, carry)

    lax.fori_loop(0, chans, fill, 0)
    first = lax.broadcasted_iota(jnp.int32, (16, LAGS), 0) == 0
    head = lag_table[0, :16, :].astype(F32)
    lag_table[0, :16, :] = jnp.where(first, 0.5 * head, head).astype(BF16)

    valid = validity[...].astype(F32).astype(BF16)
    all_segs, all_chans = valid.shape

    def iota(shape, axis):
        return lax.broadcasted_iota(jnp.int32, shape, axis)

    def gate_of(row_seg, row_chan, rows):
        seg_hot = (iota((rows, all_segs), 1) == row_seg).astype(F32).astype(BF16)
        chan_hot = (iota((rows, all_chans), 1) == row_chan).astype(F32)
        return jnp.sum(dot(seg_hot, valid) * chan_hot, axis=1, keepdims=True)

    r32 = iota((32, 1), 0)
    own_gate = gate_of(4 * seg + r32 // 8, 8 * me + r32 % 8, 32)
    r16 = iota((16, 1), 0)
    names = jnp.zeros((16, 1), jnp.int32)
    for s in range(8):
        names = jnp.where(r16 % 8 == s, sources[8 * chip + s], names)
    src_gate = gate_of(4 * seg + 2 * core + r16 // 8, names, 16)
    names = jnp.zeros((8, 1), jnp.int32)
    r8 = iota((8, 1), 0)
    for s in range(8):
        names = jnp.where(r8 == s, sources[8 * seg + s], names)
    want = (iota((8, all_chans), 1) == names).astype(F32).astype(BF16)
    want_valid = lax.dot_general(
        want, valid, (((1,), (1,)), ((), ())), preferred_element_type=F32
    ).astype(BF16)
    pairs_all = dot(want_valid, valid)
    shift_hot = (iota((all_chans, 128), 0) == 8 * me + iota((all_chans, 128), 1)).astype(F32)
    pairs = dot(pairs_all.astype(BF16), shift_hot.astype(BF16))
    bins_total = chans * block_len // 2
    scale = 1.0 / jnp.sqrt(2.0 * bins_total * jnp.maximum(pairs, 1.0))

    spread = (
        (iota((256, 256), 0) // 8 == iota((256, 256), 1) // 8).astype(F32).astype(BF16)
    )

    pad = jnp.zeros((h_hi.shape[1], 128), BF16)
    for k in range(chans):
        h_hi[k, :, 384:512] = pad
        h_hi[k, :, 896:1024] = pad
        h_lo[k, :, 384:512] = pad
        h_lo[k, :, 896:1024] = pad

    tiles = [(a, min(a + 128, block_len)) for a in range(0, block_len, 128)]

    def transform(recv, rows, gate, store):
        def sixteen(i, carry):
            r = pl.multiple_of(i * 16, 16)
            for a, b in tiles:
                xs = [
                    recv[p, pl.ds(2 * i, 2), :, a:b].reshape(16, b - a) for p in range(chans)
                ]
                half = real_dft(xs)
                for k in range(chans):
                    g = half[k] if k <= chans // 2 else conj(half[chans - k])
                    re, im = g
                    if k > 0:
                        c = twist[0, k : k + 1, a:b]
                        s = twist[1, k : k + 1, a:b]
                        if im is None:
                            re, im = re * c, -(re * s)
                        else:
                            re, im = re * c + im * s, im * c - re * s
                    elif im is None:
                        im = jnp.zeros_like(re)
                    hi, lo = split(re)
                    h_hi[k, pl.ds(r, 16), a:b] = hi
                    h_lo[k, pl.ds(r, 16), a:b] = lo
                    hi, lo = split(im)
                    h_hi[k, pl.ds(r, 16), 512 + a : 512 + b] = hi
                    h_lo[k, pl.ds(r, 16), 512 + a : 512 + b] = lo
            return carry

        lax.fori_loop(0, rows // 16, sixteen, 0)

        def second(k, total):
            hi = h_hi[k, :rows, :]
            lo = h_lo[k, :rows, :]
            x = dot(hi, table_hi[...]) + dot(lo, table_hi[...]) + dot(hi, table_lo[...])
            spec[k, :rows, :] = x
            re, im = x[:, :256], x[:, 256:]
            return total + jnp.sqrt(re * re + im * im)

        total = lax.fori_loop(0, chans, second, jnp.zeros((rows, 256), F32))
        hi, lo = split(total)
        level = (dot(hi, spread) + dot(lo, spread)) * (1.0 / 128.0) + EPSILON
        factor = gate / level

        def whiten(k, carry):
            store(k, spec[k, :rows, :256] * factor, spec[k, :rows, 256:] * factor)
            return carry

        lax.fori_loop(0, chans, whiten, 0)

    def store_src(k, re, im):
        gathered[me, k, :, :256] = re.astype(BF16)
        gathered[me, k, :, 256:] = im.astype(BF16)

    def store_own(k, re, im):
        own_white[k, :, :256] = re.astype(BF16).astype(F32)
        own_white[k, :, 256:] = im.astype(BF16).astype(F32)

    for copy in src_copies:
        copy.wait_recv()
    transform(src_recv, 16, src_gate, store_src)

    per = chans // CHUNKS
    partner = (2 * chip + 1 - core, seg)
    ag_copies = [[] for _ in range(CHUNKS)]
    fw_copies = [[] for _ in range(CHUNKS)]
    for ch in range(CHUNKS):
        for d in range(1, chips):
            ref = gathered.at[me, pl.ds(ch * per, per)]
            copy = pltpu.make_async_remote_copy(
                src_ref=ref,
                dst_ref=ref,
                send_sem=ag_ss.at[ch, d],
                recv_sem=ag_rs.at[ch, d],
                device_id=((me + 2 * d) % chans, seg),
                device_id_type=MESH,
            )
            copy.start()
            ag_copies[ch].append(copy)

    def forward(ch, d):
        slot = (me + chans - 2 * d) % chans
        ref = gathered.at[slot, pl.ds(ch * per, per)]
        copy = pltpu.make_async_remote_copy(
            src_ref=ref,
            dst_ref=ref,
            send_sem=fw_ss.at[ch, d],
            recv_sem=fw_rs.at[ch, d],
            device_id=partner,
            device_id_type=MESH,
        )
        copy.start()
        fw_copies[ch].append(copy)

    for ch in range(CHUNKS):
        forward(ch, 0)

    for copy in own_copies:
        copy.wait_recv()
    transform(own_recv, 32, own_gate, store_own)

    acc[...] = jnp.zeros_like(acc)

    def stack(k, carry):
        def octet(o, inner):
            base = pl.multiple_of(o * 64, 64)
            for l in range(2):
                re_at, im_at = l * 128, 256 + l * 128
                ar, ai = [], []
                for h in range(2):
                    re = gathered[2 * o + h, k, :, re_at : re_at + 128].astype(F32)
                    im = gathered[2 * o + h, k, :, im_at : im_at + 128].astype(F32)
                    ar += [re[:8], re[8:]]
                    ai += [im[:8], im[8:]]
                for c in range(0, 8, 2):
                    res, ims = [], []
                    for cc in (c, c + 1):
                        re = im = None
                        for g in range(4):
                            row = 8 * g + cc
                            br = own_white[k, row : row + 1, re_at : re_at + 128]
                            bi = own_white[k, row : row + 1, im_at : im_at + 128]
                            re = plus(re, ar[g] * br + ai[g] * bi)
                            im = plus(im, ar[g] * bi - ai[g] * br)
                        res.append(re)
                        ims.append(im)
                    at = pl.ds(base + 8 * c, 16)
                    prod[at, re_at : re_at + 128] = jnp.concatenate(res, 0).astype(BF16)
                    prod[at, im_at : im_at + 128] = jnp.concatenate(ims, 0).astype(BF16)
            return inner

        lax.fori_loop(0, chips, octet, 0)
        acc[...] += dot(prod[...], lag_table[k])
        return carry

    for ch in range(CHUNKS):
        for d in range(1, chips):
            ag_copies[ch][d - 1].wait_recv()
            forward(ch, d)
        for copy in fw_copies[ch]:
            copy.wait_recv()
        lax.fori_loop(ch * per, (ch + 1) * per, stack, 0)

    rs_copies = []
    for d in range(1, segs):
        to = (seg + d) % segs
        copy = pltpu.make_async_remote_copy(
            src_ref=acc.at[pl.ds(64 * to, 64)],
            dst_ref=part_recv.at[d],
            send_sem=rs_ss.at[d],
            recv_sem=rs_rs.at[d],
            device_id=(me, to),
            device_id_type=MESH,
        )
        copy.start()
        rs_copies.append(copy)
    for copy in rs_copies:
        copy.wait_recv()
    for c in range(8):
        total = acc[pl.ds(pl.multiple_of(64 * seg, 64) + 8 * c, 8), :]
        for d in range(1, segs):
            total += part_recv[d, 8 * c : 8 * c + 8, :]
        out[:, c, :] = total * scale[:, c : c + 1]

    for copy in src_copies + own_copies + rs_copies:
        copy.wait_send()
    for ch in range(CHUNKS):
        for copy in ag_copies[ch] + fw_copies[ch]:
            copy.wait_send()


def local(tables, traces, sources, validity):
    chans = lax.axis_size("chan")
    segs = lax.axis_size("seg")
    vmem = pl.BlockSpec(memory_space=pltpu.VMEM)
    block_len = traces.shape[2]
    dma = pltpu.SemaphoreType.DMA
    return pl.pallas_call(
        body,
        name="correlate",
        out_shape=jax.ShapeDtypeStruct((8, 8, LAGS), F32),
        in_specs=[pl.BlockSpec(memory_space=pltpu.SMEM)] + [vmem] * 7,
        out_specs=vmem,
        scratch_shapes=[
            pltpu.VMEM((4, 64, block_len), F32),
            pltpu.VMEM((chans, 4, 8, block_len), F32),
            pltpu.VMEM((chans, 2, 8, block_len), F32),
            pltpu.VMEM((chans, 32, 1024), BF16),
            pltpu.VMEM((chans, 32, 1024), BF16),
            pltpu.VMEM((1024, 512), BF16),
            pltpu.VMEM((1024, 512), BF16),
            pltpu.VMEM((chans, 32, 512), F32),
            pltpu.VMEM((chans, 32, 512), F32),
            pltpu.VMEM((chans, chans, 16, 512), BF16),
            pltpu.VMEM((chans, 512, LAGS), BF16),
            pltpu.VMEM((512, 512), BF16),
            pltpu.VMEM((512, LAGS), F32),
            pltpu.VMEM((segs, 64, LAGS), F32),
            dma((chans,)),
            dma((chans,)),
            dma((chans,)),
            dma((chans,)),
            dma((CHUNKS, chans // 2)),
            dma((CHUNKS, chans // 2)),
            dma((CHUNKS, chans // 2)),
            dma((CHUNKS, chans // 2)),
            dma((segs,)),
            dma((segs,)),
        ],
        compiler_params=pltpu.CompilerParams(
            collective_id=0, has_side_effects=True, vmem_limit_bytes=60 * 1024 * 1024
        ),
    )(sources, traces, validity, *[jnp.asarray(t) for t in tables])


def solution(mesh):
    chans = mesh.shape["chan"]
    length = 7680
    tables = constant_tables(length, chans)
    return jax.shard_map(
        functools.partial(local, tables),
        mesh=mesh,
        in_specs=(P("seg", None, "chan"), P(), P()),
        out_specs=P("seg", "chan", None),
        check_vma=False,
    )
```

```python
import functools
import math

import jax
import jax.numpy as jnp
import numpy as np
from jax import lax
from jax.experimental import pallas as pl
from jax.experimental.pallas import tpu as pltpu
from jax.sharding import PartitionSpec as P

LAGS = 512
EPSILON = 1e-06
MESH = pl.DeviceIdType.MESH
CHUNKS = 8
X_FIRST = (1, 4, 7)
STEPS = 32000.0
F32 = jnp.float32
BF16 = jnp.bfloat16


def constant_tables(length, blocks):
    block_len = length // blocks
    half = block_len // 2
    q = np.arange(block_len)[:, None]
    k1 = np.arange(blocks)[:, None]
    k2 = np.arange(half)[None, :]
    angle = 2.0 * math.pi / length * ((k1 * q.T) % length)
    twist = np.zeros((2, blocks, 512), np.float32)
    twist[0, :, :block_len] = np.cos(angle)
    twist[1, :, :block_len] = np.sin(angle)
    angle = 2.0 * math.pi / block_len * ((q * k2) % block_len)
    second = np.zeros((2, 512, 256), np.float32)
    second[0, :block_len, :half] = np.cos(angle)
    second[1, :block_len, :half] = np.sin(angle)
    second_hi = second.astype(jnp.bfloat16)
    second_lo = (second - second_hi.astype(np.float32)).astype(jnp.bfloat16)
    lag = (np.arange(LAGS) - LAGS // 2)[None, :]
    angle = 2.0 * math.pi / length * ((k1 * lag) % length)
    lag_one = np.stack([np.cos(angle), np.sin(angle)]).astype(np.float32)
    angle = 2.0 * math.pi / block_len * ((k2.T * lag) % block_len)
    lag_two = np.zeros((2, 256, LAGS), np.float32)
    lag_two[0, :half] = 2.0 * np.cos(angle)
    lag_two[1, :half] = 2.0 * np.sin(angle)
    return twist, second_hi, second_lo, lag_one, lag_two


def times_root(value, k, n):
    re, im = value
    c, s = math.cos(2.0 * math.pi * k / n), math.sin(2.0 * math.pi * k / n)
    if k == 0:
        return value
    if 4 * k == n:
        return (im, -re)
    if 2 * k == n:
        return (-re, None if im is None else -im)
    if im is None:
        return (re * c, re * (-s))
    return (re * c + im * s, im * c - re * s)


def plus(a, b):
    if a is None:
        return b
    return a if b is None else a + b


def conj(value):
    re, im = value
    return (re, None if im is None else -im)


def real_dft(xs):
    n = len(xs)
    if n == 2:
        return [(xs[0] + xs[1], None), (xs[0] - xs[1], None)]
    even, odd = real_dft(xs[0::2]), real_dft(xs[1::2])
    h = n // 2
    out = []
    for k in range(h + 1):
        i = k % h
        e = even[i] if i <= h // 2 else conj(even[h - i])
        o = odd[i] if i <= h // 2 else conj(odd[h - i])
        t = times_root(o, k, n)
        out.append((plus(e[0], t[0]), plus(e[1], t[1])))
    return out


def split(value):
    hi = value.astype(BF16)
    return hi, (value - hi.astype(F32)).astype(BF16)


def dot(a, b):
    return jnp.dot(a, b, preferred_element_type=F32)


def body(
    sources,
    traces,
    validity,
    twist,
    second_hi,
    second_lo,
    lag_one,
    lag_two,
    out,
    own_send,
    src_send,
    own_recv,
    src_recv,
    h_hi,
    h_lo,
    table_hi,
    table_lo,
    spec,
    white,
    mine,
    gathered,
    lag_table,
    prod_a,
    prod_b,
    acc,
    part_send,
    part_recv,
    own_ss,
    own_rs,
    src_ss,
    src_rs,
    ag_ss,
    fw_ss,
    ag_rs,
    wh_sem,
    rs_ss,
    rs_rs,
):
    chans = lax.axis_size("chan")
    segs = lax.axis_size("seg")
    me = lax.axis_index("chan")
    seg = lax.axis_index("seg")
    chip = me // 2
    core = me % 2
    z = chip // 2
    plane = chip % 2
    zs = chans // 4
    block_len = traces.shape[1]
    partner = (2 * chip + 1 - core, seg)

    def iota(shape, axis):
        return lax.broadcasted_iota(jnp.int32, shape, axis)

    def remote(src, dst, send, recv, to):
        return pltpu.make_async_remote_copy(
            src_ref=src,
            dst_ref=dst,
            send_sem=send,
            recv_sem=recv,
            device_id=to,
            device_id_type=MESH,
        )

    def device(zz, pp, cc):
        return ((zz % zs) * 4 + pp * 2 + cc, seg)

    barrier = pltpu.get_barrier_semaphore()
    for d in range(1, chans):
        pl.semaphore_signal(
            barrier, inc=1, device_id=((me + d) % chans, seg), device_id_type=MESH
        )
    for d in range(1, segs):
        for c in range(2):
            pl.semaphore_signal(
                barrier,
                inc=1,
                device_id=(2 * chip + c, (seg + d) % segs),
                device_id_type=MESH,
            )

    all_chans = traces.shape[2]
    count = 8 * chans // 2
    names = jnp.zeros((count, 1), jnp.int32)
    r_names = iota((count, 1), 0)
    for s in range(count):
        names = jnp.where(r_names == s, sources[s], names)
    row = iota((all_chans, 1), 0)
    pick = jnp.concatenate([row, names], 0)
    pick = (iota((all_chans + count, all_chans), 1) == pick).astype(F32).astype(BF16)

    def steps_of(g):
        x = traces[g]
        top = jnp.maximum(jnp.max(jnp.abs(x), axis=0, keepdims=True), 1e-30)
        power = jnp.ceil(jnp.log(top) * (128.0 / math.log(2.0))) + 1.0
        steps = jnp.round(x * (STEPS / jnp.exp2(power * (1.0 / 128.0))))
        tail = jnp.where(iota((512 - block_len, all_chans), 0) == 0, power, 0.0)
        steps = jnp.concatenate([steps, tail], 0)
        high = jnp.round(steps * (1.0 / 256.0))
        low = steps - 256.0 * high
        dims = (((1,), (1,)), ((), ()))
        return 256.0 * lax.dot_general(
            pick, high.astype(BF16), dims, preferred_element_type=F32
        ) + lax.dot_general(pick, low.astype(BF16), dims, preferred_element_type=F32)

    for i in range(2):
        pair = [steps_of(2 * i + gg).reshape(-1, 8, 512) for gg in range(2)]
        both = jnp.concatenate(pair, axis=1).astype(jnp.int32).astype(jnp.int16)
        own_send[:, i] = both[:chans]
        src_send[i] = both[chans:]

    pl.semaphore_wait(barrier, chans - 1 + 2 * (segs - 1))

    src_copies, own_copies = [], []
    for d in range(1, chans):
        to = (me + d) % chans
        copy = remote(
            src_send.at[to % 2, to // 2],
            src_recv.at[me, 0],
            src_ss.at[d],
            src_rs.at[d],
            (to, seg),
        )
        copy.start()
        src_copies.append(copy)
    for d in range(1, chans):
        to = (me + d) % chans
        copy = remote(
            own_send.at[to], own_recv.at[me], own_ss.at[d], own_rs.at[d], (to, seg)
        )
        copy.start()
        own_copies.append(copy)
    src_recv[pl.ds(me, 1), 0] = src_send[core, pl.ds(chip, 1)]
    own_recv[pl.ds(me, 1)] = own_send[pl.ds(me, 1)]

    table_hi[:512, :256] = second_hi[0]
    table_hi[512:, :256] = second_hi[1]
    table_hi[:512, 256:] = -second_hi[1]
    table_hi[512:, 256:] = second_hi[0]
    table_lo[:512, :256] = second_lo[0]
    table_lo[512:, :256] = second_lo[1]
    table_lo[:512, 256:] = -second_lo[1]
    table_lo[512:, 256:] = second_lo[0]

    def fill(k1, carry):
        c1 = lag_one[0, pl.ds(k1, 1), :]
        s1 = lag_one[1, pl.ds(k1, 1), :]

        def rows(i, inner):
            r = pl.multiple_of(i * 16, 16)
            c2 = lag_two[0, pl.ds(r, 16), :]
            s2 = lag_two[1, pl.ds(r, 16), :]
            lag_table[k1, pl.ds(r, 16), :] = (c1 * c2 - s1 * s2).astype(BF16)
            lag_table[k1, pl.ds(r + 256, 16), :] = (-(s1 * c2 + c1 * s2)).astype(BF16)
            return inner

        return lax.fori_loop(0, 16, rows, carry)

    lax.fori_loop(0, chans, fill, 0)
    first = iota((16, LAGS), 0) == 0
    head = lag_table[0, :16, :].astype(F32)
    lag_table[0, :16, :] = jnp.where(first, 0.5 * head, head).astype(BF16)

    valid = validity[...].astype(F32).astype(BF16)
    all_segs = valid.shape[0]

    def gate_of(row_seg, row_chan, rows):
        seg_hot = (iota((rows, all_segs), 1) == row_seg).astype(F32).astype(BF16)
        chan_hot = (iota((rows, all_chans), 1) == row_chan).astype(F32)
        return jnp.sum(dot(seg_hot, valid) * chan_hot, axis=1, keepdims=True)

    def named(r, base):
        found = jnp.zeros(r.shape, jnp.int32)
        for s in range(8):
            found = jnp.where(r == s, sources[8 * base + s], found)
        return found

    r32 = iota((32, 1), 0)
    own_gate = gate_of(4 * seg + r32 // 8, 8 * me + r32 % 8, 32)
    r16 = iota((16, 1), 0)
    src_gate = gate_of(4 * seg + 2 * core + r16 // 8, named(r16 % 8, chip), 16)
    want = iota((8, all_chans), 1) == named(iota((8, 1), 0), seg)
    want_valid = lax.dot_general(
        want.astype(F32).astype(BF16),
        valid,
        (((1,), (1,)), ((), ())),
        preferred_element_type=F32,
    ).astype(BF16)
    pairs_all = dot(want_valid, valid)
    shift_hot = (iota((all_chans, 128), 0) == 8 * me + iota((all_chans, 128), 1)).astype(F32)
    pairs = dot(pairs_all.astype(BF16), shift_hot.astype(BF16))
    bins_total = chans * block_len // 2
    scale = 1.0 / jnp.sqrt(2.0 * bins_total * jnp.maximum(pairs, 1.0))

    spread = (iota((256, 256), 0) // 8 == iota((256, 256), 1) // 8).astype(F32).astype(BF16)

    def transform(recv, groups, gate, store):
        rows = 16 * groups

        def sixteen(i, carry):
            units = []
            for p in range(chans):
                last = recv[p, i, :, 384:512].astype(jnp.int32).astype(F32)
                at = block_len - 384
                units.append(jnp.exp2(last[:, at : at + 1] * (1.0 / 128.0)) * (1.0 / STEPS))
            for a in range(0, 512, 128):
                xs = [
                    recv[p, i, :, a : a + 128].astype(jnp.int32).astype(F32) * units[p]
                    for p in range(chans)
                ]
                half = real_dft(xs)
                for k in range(chans):
                    g = half[k] if k <= chans // 2 else conj(half[chans - k])
                    re, im = g
                    c = twist[0, k : k + 1, a : a + 128]
                    s = twist[1, k : k + 1, a : a + 128]
                    if im is None:
                        re, im = re * c, -(re * s)
                    else:
                        re, im = re * c + im * s, im * c - re * s
                    at = pl.ds(pl.multiple_of(k * rows + 16 * i, 16), 16)
                    hi, lo = split(re)
                    h_hi[at, a : a + 128] = hi
                    h_lo[at, a : a + 128] = lo
                    hi, lo = split(im)
                    h_hi[at, 512 + a : 640 + a] = hi
                    h_lo[at, 512 + a : 640 + a] = lo
            return carry

        lax.fori_loop(0, groups, sixteen, 0)

        def second(m, carry):
            at = pl.ds(pl.multiple_of(m * 256, 256), 256)
            hi = h_hi[at, :]
            spec[at, :] = (
                dot(hi, table_hi[...]) + dot(h_lo[at, :], table_hi[...]) + dot(hi, table_lo[...])
            )
            return carry

        lax.fori_loop(0, chans * rows // 256, second, 0)

        def level(k, total):
            at = pl.ds(pl.multiple_of(k * rows, rows), rows)
            re, im = spec[at, :256], spec[at, 256:]
            return total + jnp.sqrt(re * re + im * im)

        total = lax.fori_loop(0, chans, level, jnp.zeros((rows, 256), F32))
        hi, lo = split(total)
        mean = (dot(hi, spread) + dot(lo, spread)) * (1.0 / 128.0) + EPSILON
        factor = gate / mean

        def whiten(k, carry):
            at = pl.ds(pl.multiple_of(k * rows, rows), rows)
            store(k, spec[at, :256] * factor, spec[at, 256:] * factor)
            return carry

        lax.fori_loop(0, chans, whiten, 0)

    def store_src(k, re, im):
        mine[k, :, :256] = re.astype(BF16)
        mine[k, :, 256:] = im.astype(BF16)

    def store_own(k, re, im):
        white[core, k, :, :256] = re.astype(BF16).astype(F32)
        white[core, k, :, 256:] = im.astype(BF16).astype(F32)

    for copy in src_copies:
        copy.wait_recv()
    transform(src_recv, 1, src_gate, store_src)

    per = chans // CHUNKS
    home = core == plane
    slot = 2 * z + core

    def span(ch):
        return pl.ds(ch * per, per)

    def direct(ch, t):
        if t == 0:
            to = partner
        elif t < zs:
            to = device(z + t, plane, plane)
        else:
            to = device(z, 1 - plane, plane)
        return remote(
            mine.at[span(ch)],
            gathered.at[slot, span(ch)],
            ag_ss.at[ch, t],
            ag_rs.at[ch, slot],
            to,
        )

    def slot_of(d, e):
        return 2 * ((z + d) % zs) + (core + e) % 2

    def onward(ch, t):
        d, e = 1 + t // 2, t % 2
        if ch in X_FIRST:
            at, to = slot_of(0, e), device(z + d, plane, core)
        else:
            at, to = slot_of(d, e), device(z, 1 - plane, core)
        ref = gathered.at[at, span(ch)]
        return remote(ref, ref, fw_ss.at[ch, t], ag_rs.at[ch, at], to)

    def arrive(ch, d, e):
        at = slot_of(d, e)
        ref = gathered.at[at, span(ch)]
        remote(ref, ref, fw_ss.at[ch, 0], ag_rs.at[ch, at], partner).wait_recv()

    for ch in range(CHUNKS):
        for t in range(zs, 0, -1):
            direct(ch, t).start()

        @pl.when(jnp.logical_not(home))
        def _(ch=ch):
            direct(ch, 0).start()

    @pl.when(home)
    def _():
        gathered[pl.ds(slot, 1)] = mine[...][None]

    for copy in own_copies:
        copy.wait_recv()
    transform(own_recv, 2, own_gate, store_own)
    white_copy = remote(white.at[core], white.at[core], wh_sem.at[0], wh_sem.at[1], partner)
    white_copy.start()

    acc[...] = jnp.zeros_like(acc)
    prod_b[...] = jnp.zeros_like(prod_b)

    def stack(k, half, prod):
        for oo in range(2):
            o = 2 * half + oo
            for l in range(2):
                re_at, im_at = l * 128, 256 + l * 128
                ar, ai = [], []
                for h in range(2):
                    re = gathered[2 * o + h, k, :, re_at : re_at + 128].astype(F32)
                    im = gathered[2 * o + h, k, :, im_at : im_at + 128].astype(F32)
                    ar += [re[:8], re[8:]]
                    ai += [im[:8], im[8:]]
                for c in range(0, 16, 2):
                    res, ims = [], []
                    for cc in (c, c + 1):
                        re = im = None
                        for g in range(4):
                            at = 8 * g + cc % 8
                            br = white[cc // 8, k, at : at + 1, re_at : re_at + 128]
                            bi = white[cc // 8, k, at : at + 1, im_at : im_at + 128]
                            re = plus(re, ar[g] * br + ai[g] * bi)
                            im = plus(im, ar[g] * bi - ai[g] * br)
                        res.append(re)
                        ims.append(im)
                    at = 128 * oo + 8 * c
                    prod[at : at + 16, re_at : re_at + 128] = jnp.concatenate(res, 0).astype(BF16)
                    prod[at : at + 16, im_at : im_at + 128] = jnp.concatenate(ims, 0).astype(BF16)

    def step(k, carry):
        acc[256:] += dot(prod_b[...], lag_table[jnp.maximum(k - 1, 0)])
        stack(k, 0, prod_a)
        acc[:256] += dot(prod_a[...], lag_table[k])
        stack(k, 1, prod_b)
        return carry

    forwards = 2 * (zs - 1)

    def take(ch, early):
        x_first = ch in X_FIRST

        @pl.when(home)
        def _():
            for d in range(1, zs):
                for e in range(2):
                    if early == (not x_first):
                        arrive(ch, d, e)
                        if early:
                            onward(ch, 2 * (d - 1) + e).start()
            if not early:
                arrive(ch, 0, 1)

        @pl.when(jnp.logical_not(home))
        def _():
            if early == x_first:
                for e in range(2):
                    arrive(ch, 0, e)
            if early and x_first:
                for t in range(forwards):
                    onward(ch, t).start()
            if not early:
                for d in range(1, zs):
                    for e in range(2):
                        arrive(ch, d, e)

    take(0, True)
    white_copy.wait_recv()
    for ch in range(CHUNKS):
        if ch + 1 < CHUNKS:
            take(ch + 1, True)
        take(ch, False)
        lax.fori_loop(ch * per, (ch + 1) * per, step, 0)
    acc[256:] += dot(prod_b[...], lag_table[chans - 1])

    part_send[...] = acc[...].astype(BF16)

    def partial(o, c):
        rows = part_send.at[128 * o + 64 * c : 128 * o + 64 * c + 64]
        to = (2 * chip + c, 2 * o + core)
        return remote(rows, part_recv.at[seg], rs_ss.at[o, c], rs_rs.at[seg], to)

    def remains(o, c):
        return jnp.logical_and(core == c, seg == 2 * o + core)

    for o in range(zs):
        for c in range(2):

            @pl.when(jnp.logical_not(remains(o, c)))
            def _(o=o, c=c):
                partial(o, c).start()

            @pl.when(remains(o, c))
            def _(o=o, c=c):
                part_recv[pl.ds(seg, 1)] = part_send[
                    128 * o + 64 * c : 128 * o + 64 * c + 64
                ][None]

    def landed(d):
        at = (seg + d) % segs
        ref = part_recv.at[at]
        remote(ref, ref, rs_ss.at[0, 0], rs_rs.at[at], partner).wait_recv()

    @pl.when(seg % 2 != core)
    def _():
        landed(0)

    for d in range(1, segs):
        landed(d)
    for c in range(8):
        total = part_recv[0, 8 * c : 8 * c + 8, :].astype(F32)
        for j in range(1, segs):
            total += part_recv[j, 8 * c : 8 * c + 8, :].astype(F32)
        out[:, c, :] = total * scale[:, c : c + 1]

    for copy in src_copies + own_copies:
        copy.wait_send()
    white_copy.wait_send()
    for ch in range(CHUNKS):
        for t in range(1, zs + 1):
            direct(ch, t).wait_send()

        @pl.when(jnp.logical_not(home))
        def _(ch=ch):
            direct(ch, 0).wait_send()

        @pl.when(home != (ch in X_FIRST))
        def _(ch=ch):
            for t in range(forwards):
                onward(ch, t).wait_send()

    for o in range(zs):
        for c in range(2):

            @pl.when(jnp.logical_not(remains(o, c)))
            def _(o=o, c=c):
                partial(o, c).wait_send()


def local(tables, traces, sources, validity):
    chans = lax.axis_size("chan")
    segs = lax.axis_size("seg")
    vmem = pl.BlockSpec(memory_space=pltpu.VMEM)
    dma = pltpu.SemaphoreType.DMA
    return pl.pallas_call(
        body,
        name="correlate",
        out_shape=jax.ShapeDtypeStruct((8, 8, LAGS), F32),
        in_specs=[pl.BlockSpec(memory_space=pltpu.SMEM)] + [vmem] * 7,
        out_specs=vmem,
        scratch_shapes=[
            pltpu.VMEM((chans, 2, 16, 512), jnp.int16),
            pltpu.VMEM((2, chans // 2, 16, 512), jnp.int16),
            pltpu.VMEM((chans, 2, 16, 512), jnp.int16),
            pltpu.VMEM((chans, 1, 16, 512), jnp.int16),
            pltpu.VMEM((32 * chans, 1024), BF16),
            pltpu.VMEM((32 * chans, 1024), BF16),
            pltpu.VMEM((1024, 512), BF16),
            pltpu.VMEM((1024, 512), BF16),
            pltpu.VMEM((32 * chans, 512), F32),
            pltpu.VMEM((2, chans, 32, 512), F32),
            pltpu.VMEM((chans, 16, 512), BF16),
            pltpu.VMEM((8, chans, 16, 512), BF16),
            pltpu.VMEM((chans, 512, LAGS), BF16),
            pltpu.VMEM((256, 512), BF16),
            pltpu.VMEM((256, 512), BF16),
            pltpu.VMEM((512, LAGS), F32),
            pltpu.VMEM((512, LAGS), BF16),
            pltpu.VMEM((segs, 64, LAGS), BF16),
            dma((chans,)),
            dma((chans,)),
            dma((chans,)),
            dma((chans,)),
            dma((CHUNKS, 5)),
            dma((CHUNKS, 6)),
            dma((CHUNKS, 8)),
            dma((2,)),
            dma((4, 2)),
            dma((segs,)),
        ],
        compiler_params=pltpu.CompilerParams(
            collective_id=0, has_side_effects=True, vmem_limit_bytes=60 * 1024 * 1024
        ),
    )(sources, traces.transpose(0, 2, 1), validity, *[jnp.asarray(t) for t in tables])


def solution(mesh):
    chans = mesh.shape["chan"]
    length = 7680
    tables = constant_tables(length, chans)
    return jax.shard_map(
        functools.partial(local, tables),
        mesh=mesh,
        in_specs=(P("seg", None, "chan"), P(), P()),
        out_specs=P("seg", "chan", None),
        check_vma=False,
    )
```

```python
import functools
import math

import jax
import jax.numpy as jnp
import numpy as np
from jax import lax
from jax.experimental import pallas as pl
from jax.experimental.pallas import tpu as pltpu
from jax.sharding import PartitionSpec as P

LAGS = 512
EPSILON = 1e-06
MESH = pl.DeviceIdType.MESH
CHUNKS = 8
STEPS = 32000.0
F32 = jnp.float32
BF16 = jnp.bfloat16


def constant_tables(length, blocks):
    block_len = length // blocks
    half = block_len // 2
    q = np.arange(block_len)[:, None]
    k1 = np.arange(blocks)[:, None]
    k2 = np.arange(half)[None, :]
    angle = 2.0 * math.pi / length * ((k1 * q.T) % length)
    twist = np.zeros((2, blocks, 512), np.float32)
    twist[0, :, :block_len] = np.cos(angle)
    twist[1, :, :block_len] = np.sin(angle)
    angle = 2.0 * math.pi / block_len * ((q * k2) % block_len)
    second = np.zeros((2, 512, 256), np.float32)
    second[0, :block_len, :half] = np.cos(angle)
    second[1, :block_len, :half] = np.sin(angle)
    second_hi = second.astype(jnp.bfloat16)
    second_lo = (second - second_hi.astype(np.float32)).astype(jnp.bfloat16)
    lag = (np.arange(LAGS) - LAGS // 2)[None, :]
    angle = 2.0 * math.pi / length * ((k1 * lag) % length)
    lag_one = np.stack([np.cos(angle), np.sin(angle)]).astype(np.float32)
    angle = 2.0 * math.pi / block_len * ((k2.T * lag) % block_len)
    lag_two = np.zeros((2, 256, LAGS), np.float32)
    lag_two[0, :half] = 2.0 * np.cos(angle)
    lag_two[1, :half] = 2.0 * np.sin(angle)
    return twist, second_hi, second_lo, lag_one, lag_two


def times_root(value, k, n):
    re, im = value
    c, s = math.cos(2.0 * math.pi * k / n), math.sin(2.0 * math.pi * k / n)
    if k == 0:
        return value
    if 4 * k == n:
        return (im, -re)
    if 2 * k == n:
        return (-re, None if im is None else -im)
    if im is None:
        return (re * c, re * (-s))
    return (re * c + im * s, im * c - re * s)


def plus(a, b):
    if a is None:
        return b
    return a if b is None else a + b


def conj(value):
    re, im = value
    return (re, None if im is None else -im)


def real_dft(xs):
    n = len(xs)
    if n == 2:
        return [(xs[0] + xs[1], None), (xs[0] - xs[1], None)]
    even, odd = real_dft(xs[0::2]), real_dft(xs[1::2])
    h = n // 2
    out = []
    for k in range(h + 1):
        i = k % h
        e = even[i] if i <= h // 2 else conj(even[h - i])
        o = odd[i] if i <= h // 2 else conj(odd[h - i])
        t = times_root(o, k, n)
        out.append((plus(e[0], t[0]), plus(e[1], t[1])))
    return out


def split(value):
    hi = value.astype(BF16)
    return hi, (value - hi.astype(F32)).astype(BF16)


def dot(a, b):
    return jnp.dot(a, b, preferred_element_type=F32)


def body(
    sources,
    traces,
    validity,
    twist_in,
    second_hi,
    second_lo,
    lag_one,
    lag_two,
    out,
    names_smem,
    staged,
    valid_in,
    twist,
    sec_hi,
    sec_lo,
    one,
    two,
    own_send,
    src_send,
    own_recv,
    src_recv,
    h_hi,
    h_lo,
    table_hi,
    table_lo,
    spec,
    white,
    white_send,
    white_recv,
    gathered,
    lag_table,
    prod_a,
    prod_b,
    acc,
    part_send,
    part_recv,
    in_sem,
    own_ss,
    own_rs,
    src_ss,
    src_rs,
    ag_ss,
    fw_ss,
    ag_rs,
    wh_ss,
    wh_rs,
    rs_ss,
    rs_rs,
):
    chans = lax.axis_size("chan")
    segs = lax.axis_size("seg")
    me = lax.axis_index("chan")
    seg = lax.axis_index("seg")
    chip = me // 2
    core = me % 2
    z = chip // 2
    plane = chip % 2
    zs = chans // 4
    block_len = traces.shape[1]
    partner = (2 * chip + 1 - core, seg)

    def iota(shape, axis):
        return lax.broadcasted_iota(jnp.int32, shape, axis)

    def remote(src, dst, send, recv, to):
        return pltpu.make_async_remote_copy(
            src_ref=src,
            dst_ref=dst,
            send_sem=send,
            recv_sem=recv,
            device_id=to,
            device_id_type=MESH,
        )

    def device(zz, pp, cc):
        return (zz % zs) * 4 + pp * 2 + cc

    def octet_of(zz, pp):
        return 2 * zz + (zz + pp) % 2

    fetch = [
        pltpu.make_async_copy(a, b, in_sem.at[n])
        for n, (a, b) in enumerate(
            [(traces.at[g], staged.at[g]) for g in range(4)]
            + [
                (sources, names_smem),
                (validity, valid_in),
                (twist_in, twist),
                (second_hi, sec_hi),
                (second_lo, sec_lo),
                (lag_one, one),
                (lag_two, two),
            ]
        )
    ]
    for n in (4, 0, 1, 2, 3, 7, 8, 9, 10, 5, 6):
        fetch[n].start()

    barrier = pltpu.get_barrier_semaphore()
    for d in range(1, chans):
        pl.semaphore_signal(
            barrier, inc=1, device_id=((me + d) % chans, seg), device_id_type=MESH
        )
    for d in range(1, segs):
        for p in range(2):
            pl.semaphore_signal(
                barrier,
                inc=1,
                device_id=(device(z, p, core), (seg + d) % segs),
                device_id_type=MESH,
            )

    fetch[4].wait()
    all_chans = staged.shape[2]
    count = 8 * chans // 2
    names = jnp.zeros((count, 1), jnp.int32)
    r_names = iota((count, 1), 0)
    for s in range(count):
        names = jnp.where(r_names == s, names_smem[s], names)
    row = iota((all_chans, 1), 0)
    pick = jnp.concatenate([row, names], 0)
    pick = (iota((all_chans + count, all_chans), 1) == pick).astype(F32).astype(BF16)

    def steps_of(g):
        fetch[g].wait()
        x = staged[g]
        top = jnp.maximum(jnp.max(jnp.abs(x), axis=0, keepdims=True), 1e-30)
        power = jnp.ceil(jnp.log(top) * (128.0 / math.log(2.0))) + 1.0
        steps = jnp.round(x * (STEPS / jnp.exp2(power * (1.0 / 128.0))))
        tail = jnp.where(iota((512 - block_len, all_chans), 0) == 0, power, 0.0)
        steps = jnp.concatenate([steps, tail], 0)
        high = jnp.round(steps * (1.0 / 256.0))
        low = steps - 256.0 * high
        dims = (((1,), (1,)), ((), ()))
        return 256.0 * lax.dot_general(
            pick, high.astype(BF16), dims, preferred_element_type=F32
        ) + lax.dot_general(pick, low.astype(BF16), dims, preferred_element_type=F32)

    for i in range(2):
        pair = [steps_of(2 * i + gg).reshape(-1, 8, 512) for gg in range(2)]
        both = jnp.concatenate(pair, axis=1).astype(jnp.int32).astype(jnp.int16)
        own_send[i] = both[:chans]
        src_send[i] = both[chans:]

    pl.semaphore_wait(barrier, chans - 1 + 2 * (segs - 1))

    src_copies, own_copies = [], [[], []]
    for d in range(1, chans):
        to = (me + d) % chans
        copy = remote(
            src_send.at[to % 2, octet_of(to // 4, (to // 2) % 2)],
            src_recv.at[me],
            src_ss.at[d],
            src_rs.at[d],
            (to, seg),
        )
        copy.start()
        src_copies.append(copy)
    for i in range(2):
        for d in range(1, chans):
            to = (me + d) % chans
            copy = remote(
                own_send.at[i, to],
                own_recv.at[i, me],
                own_ss.at[i, d],
                own_rs.at[i, d],
                (to, seg),
            )
            copy.start()
            own_copies[i].append(copy)
    src_recv[pl.ds(me, 1)] = src_send[core, pl.ds(octet_of(z, plane), 1)]
    for i in range(2):
        own_recv[i, pl.ds(me, 1)] = own_send[i, pl.ds(me, 1)]

    for n in range(5, 11):
        fetch[n].wait()

    table_hi[:512, :256] = sec_hi[0]
    table_hi[512:, :256] = sec_hi[1]
    table_hi[:512, 256:] = -sec_hi[1]
    table_hi[512:, 256:] = sec_hi[0]
    table_lo[:512, :256] = sec_lo[0]
    table_lo[512:, :256] = sec_lo[1]
    table_lo[:512, 256:] = -sec_lo[1]
    table_lo[512:, 256:] = sec_lo[0]

    def fill(k1, carry):
        c1 = one[0, pl.ds(k1, 1), :]
        s1 = one[1, pl.ds(k1, 1), :]

        def rows(i, inner):
            r = pl.multiple_of(i * 16, 16)
            c2 = two[0, pl.ds(r, 16), :]
            s2 = two[1, pl.ds(r, 16), :]
            lag_table[k1, pl.ds(r, 16), :] = (c1 * c2 - s1 * s2).astype(BF16)
            lag_table[k1, pl.ds(r + 256, 16), :] = (-(s1 * c2 + c1 * s2)).astype(BF16)
            return inner

        return lax.fori_loop(0, 16, rows, carry)

    lax.fori_loop(0, chans, fill, 0)
    first = iota((16, LAGS), 0) == 0
    head = lag_table[0, :16, :].astype(F32)
    lag_table[0, :16, :] = jnp.where(first, 0.5 * head, head).astype(BF16)

    valid = valid_in[...].astype(F32).astype(BF16)
    all_segs = valid.shape[0]

    def gate_of(row_seg, row_chan, rows):
        seg_hot = (iota((rows, all_segs), 1) == row_seg).astype(F32).astype(BF16)
        chan_hot = (iota((rows, all_chans), 1) == row_chan).astype(F32)
        return jnp.sum(dot(seg_hot, valid) * chan_hot, axis=1, keepdims=True)

    def named(r, base):
        found = jnp.zeros(r.shape, jnp.int32)
        for s in range(8):
            found = jnp.where(r == s, names_smem[8 * base + s], found)
        return found

    r16 = iota((16, 1), 0)
    own_gates = [
        gate_of(4 * seg + 2 * i + r16 // 8, 8 * me + r16 % 8, 16) for i in range(2)
    ]
    src_gate = gate_of(4 * seg + 2 * core + r16 // 8, named(r16 % 8, octet_of(z, plane)), 16)
    want = iota((8, all_chans), 1) == named(iota((8, 1), 0), seg)
    want_valid = lax.dot_general(
        want.astype(F32).astype(BF16),
        valid,
        (((1,), (1,)), ((), ())),
        preferred_element_type=F32,
    ).astype(BF16)
    pairs_all = dot(want_valid, valid)
    shift_hot = (iota((all_chans, 128), 0) == 8 * me + iota((all_chans, 128), 1)).astype(F32)
    pairs = dot(pairs_all.astype(BF16), shift_hot.astype(BF16))
    bins_total = chans * block_len // 2
    scale = 1.0 / jnp.sqrt(2.0 * bins_total * jnp.maximum(pairs, 1.0))

    spread = (iota((256, 256), 0) // 8 == iota((256, 256), 1) // 8).astype(F32).astype(BF16)

    def transform(recv, gate, store):
        units = []
        for p in range(chans):
            last = recv[p, :, 384:512].astype(jnp.int32).astype(F32)
            at = block_len - 384
            units.append(jnp.exp2(last[:, at : at + 1] * (1.0 / 128.0)) * (1.0 / STEPS))
        for a in range(0, 512, 128):
            xs = [
                recv[p, :, a : a + 128].astype(jnp.int32).astype(F32) * units[p]
                for p in range(chans)
            ]
            half = real_dft(xs)
            for k in range(chans):
                g = half[k] if k <= chans // 2 else conj(half[chans - k])
                re, im = g
                c = twist[0, k : k + 1, a : a + 128]
                s = twist[1, k : k + 1, a : a + 128]
                if im is None:
                    re, im = re * c, -(re * s)
                else:
                    re, im = re * c + im * s, im * c - re * s
                at = slice(16 * k, 16 * k + 16)
                hi, lo = split(re)
                h_hi[at, a : a + 128] = hi
                h_lo[at, a : a + 128] = lo
                hi, lo = split(im)
                h_hi[at, 512 + a : 640 + a] = hi
                h_lo[at, 512 + a : 640 + a] = lo
        spec[...] = (
            dot(h_hi[...], table_hi[...])
            + dot(h_lo[...], table_hi[...])
            + dot(h_hi[...], table_lo[...])
        )
        total = None
        for k in range(chans):
            re, im = spec[16 * k : 16 * k + 16, :256], spec[16 * k : 16 * k + 16, 256:]
            total = plus(total, jnp.sqrt(re * re + im * im))
        hi, lo = split(total)
        mean = (dot(hi, spread) + dot(lo, spread)) * (1.0 / 128.0) + EPSILON
        factor = gate / mean
        for k in range(chans):
            for part in range(2):
                at = slice(256 * part, 256 * part + 256)
                store(k, at, (spec[16 * k : 16 * k + 16, at] * factor).astype(BF16))

    per = chans // CHUNKS
    slot = 2 * z + core

    def span(ch):
        return pl.ds(ch * per, per)

    def store_src(k, at, value):
        gathered[slot, k, :, at] = value

    for copy in src_copies:
        copy.wait_recv()
    transform(src_recv, src_gate, store_src)

    def gather(ch, d):
        ref = gathered.at[slot, span(ch)]
        to = partner if d == 0 else (device(z + d, plane, core), seg)
        return remote(ref, ref, ag_ss.at[ch, d], ag_rs.at[ch, slot], to)

    def slot_of(d, cc):
        return 2 * ((z + d) % zs) + cc

    def forward(ch, d):
        at = slot_of(d, core)
        ref = gathered.at[at, span(ch)]
        return remote(ref, ref, fw_ss.at[ch, d], ag_rs.at[ch, at], partner)

    def arrive(ch, d, cc):
        at = slot_of(d, cc)
        ref = gathered.at[at, span(ch)]
        remote(ref, ref, fw_ss.at[ch, 0], ag_rs.at[ch, at], partner).wait_recv()

    for ch in range(CHUNKS):
        for d in range(zs - 1, -1, -1):
            gather(ch, d).start()

    across = (device(z, 1 - plane, core), seg)

    def cross(i, ch):
        return remote(
            white_send.at[i, span(ch)],
            white_recv.at[i, span(ch)],
            wh_ss.at[i, ch],
            wh_rs.at[i, ch],
            across,
        )

    for i in range(2):

        def store_own(k, at, value, i=i):
            white_send[i, k, :, at] = value
            white[plane, k, 16 * i : 16 * i + 16, at] = value.astype(F32)

        for copy in own_copies[i]:
            copy.wait_recv()
        transform(own_recv.at[i], own_gates[i], store_own)
        for ch in range(CHUNKS):
            cross(i, ch).start()

    acc[...] = jnp.zeros_like(acc)
    prod_b[...] = jnp.zeros_like(prod_b)

    def stack(k, half, prod):
        for oo in range(2):
            o = 2 * half + oo
            for l in range(2):
                re_at, im_at = l * 128, 256 + l * 128
                ar, ai = [], []
                for h in range(2):
                    re = gathered[2 * o + h, k, :, re_at : re_at + 128].astype(F32)
                    im = gathered[2 * o + h, k, :, im_at : im_at + 128].astype(F32)
                    ar += [re[:8], re[8:]]
                    ai += [im[:8], im[8:]]
                for c in range(0, 16, 2):
                    res, ims = [], []
                    for cc in (c, c + 1):
                        re = im = None
                        for g in range(4):
                            at = 8 * g + cc % 8
                            br = white[cc // 8, k, at : at + 1, re_at : re_at + 128]
                            bi = white[cc // 8, k, at : at + 1, im_at : im_at + 128]
                            re = plus(re, ar[g] * br + ai[g] * bi)
                            im = plus(im, ar[g] * bi - ai[g] * br)
                        res.append(re)
                        ims.append(im)
                    at = 128 * oo + 8 * c
                    prod[at : at + 16, re_at : re_at + 128] = jnp.concatenate(res, 0).astype(BF16)
                    prod[at : at + 16, im_at : im_at + 128] = jnp.concatenate(ims, 0).astype(BF16)

    def step(k, carry):
        acc[256:] += dot(prod_b[...], lag_table[jnp.maximum(k - 1, 0)])
        stack(k, 0, prod_a)
        acc[:256] += dot(prod_a[...], lag_table[k])
        stack(k, 1, prod_b)
        return carry


    def relay(ch):
        for d in range(1, zs):
            arrive(ch, d, core)
            forward(ch, d).start()

    def widen(k, carry):
        for i in range(2):
            white[1 - plane, k, 16 * i : 16 * i + 16, :] = white_recv[i, k].astype(F32)
        return carry

    relay(0)
    for ch in range(CHUNKS):
        if ch + 1 < CHUNKS:
            relay(ch + 1)
        for d in range(zs):
            arrive(ch, d, 1 - core)
        for i in range(2):
            cross(i, ch).wait_recv()
        lax.fori_loop(ch * per, (ch + 1) * per, widen, 0)
        lax.fori_loop(ch * per, (ch + 1) * per, step, 0)
    acc[256:] += dot(prod_b[...], lag_table[chans - 1])

    part_send[...] = acc[...].astype(BF16)

    def partial(o, p):
        rows = part_send.at[128 * o + 64 * p : 128 * o + 64 * p + 64]
        to = (device(z, p, core), octet_of(o, plane))
        return remote(rows, part_recv.at[seg], rs_ss.at[o, p], rs_rs.at[seg], to)

    def remains(o, p):
        return jnp.logical_and(plane == p, seg == octet_of(o, plane))

    for o in range(zs):
        for p in range(2):

            @pl.when(jnp.logical_not(remains(o, p)))
            def _(o=o, p=p):
                partial(o, p).start()

            @pl.when(remains(o, p))
            def _(o=o, p=p):
                part_recv[pl.ds(seg, 1)] = part_send[
                    128 * o + 64 * p : 128 * o + 64 * p + 64
                ][None]

    def landed(d):
        at = (seg + d) % segs
        ref = part_recv.at[at]
        remote(ref, ref, rs_ss.at[0, 0], rs_rs.at[at], partner).wait_recv()

    @pl.when((seg + seg // 2) % 2 != plane)
    def _():
        landed(0)

    for d in range(1, segs):
        landed(d)
    for c in range(8):
        total = part_recv[0, 8 * c : 8 * c + 8, :].astype(F32)
        for j in range(1, segs):
            total += part_recv[j, 8 * c : 8 * c + 8, :].astype(F32)
        out[:, c, :] = total * scale[:, c : c + 1]

    for copy in src_copies + own_copies[0] + own_copies[1]:
        copy.wait_send()
    for ch in range(CHUNKS):
        for d in range(zs):
            gather(ch, d).wait_send()
        for d in range(1, zs):
            forward(ch, d).wait_send()
        for i in range(2):
            cross(i, ch).wait_send()
    for o in range(zs):
        for p in range(2):

            @pl.when(jnp.logical_not(remains(o, p)))
            def _(o=o, p=p):
                partial(o, p).wait_send()


def local(tables, traces, sources, validity):
    chans = lax.axis_size("chan")
    segs = lax.axis_size("seg")
    vmem = pl.BlockSpec(memory_space=pltpu.VMEM)
    hbm = pl.BlockSpec(memory_space=pl.ANY)
    dma = pltpu.SemaphoreType.DMA
    turned = traces.transpose(0, 2, 1)
    tables = [jnp.asarray(t) for t in tables]
    return pl.pallas_call(
        body,
        name="correlate",
        out_shape=jax.ShapeDtypeStruct((8, 8, LAGS), F32),
        in_specs=[hbm] * 8,
        out_specs=vmem,
        scratch_shapes=[
            pltpu.SMEM(sources.shape, jnp.int32),
            pltpu.VMEM(turned.shape, F32),
            pltpu.VMEM(validity.shape, jnp.int32),
            *[pltpu.VMEM(t.shape, t.dtype) for t in tables],
            pltpu.VMEM((2, chans, 16, 512), jnp.int16),
            pltpu.VMEM((2, chans // 2, 16, 512), jnp.int16),
            pltpu.VMEM((2, chans, 16, 512), jnp.int16),
            pltpu.VMEM((chans, 16, 512), jnp.int16),
            pltpu.VMEM((16 * chans, 1024), BF16),
            pltpu.VMEM((16 * chans, 1024), BF16),
            pltpu.VMEM((1024, 512), BF16),
            pltpu.VMEM((1024, 512), BF16),
            pltpu.VMEM((16 * chans, 512), F32),
            pltpu.VMEM((2, chans, 32, 512), F32),
            pltpu.VMEM((2, chans, 16, 512), BF16),
            pltpu.VMEM((2, chans, 16, 512), BF16),
            pltpu.VMEM((8, chans, 16, 512), BF16),
            pltpu.VMEM((chans, 512, LAGS), BF16),
            pltpu.VMEM((256, 512), BF16),
            pltpu.VMEM((256, 512), BF16),
            pltpu.VMEM((512, LAGS), F32),
            pltpu.VMEM((512, LAGS), BF16),
            pltpu.VMEM((segs, 64, LAGS), BF16),
            dma((11,)),
            dma((2, chans)),
            dma((2, chans)),
            dma((chans,)),
            dma((chans,)),
            dma((CHUNKS, 4)),
            dma((CHUNKS, 4)),
            dma((CHUNKS, 8)),
            dma((2, CHUNKS)),
            dma((2, CHUNKS)),
            dma((4, 2)),
            dma((segs,)),
        ],
        compiler_params=pltpu.CompilerParams(
            collective_id=0, has_side_effects=True, vmem_limit_bytes=60 * 1024 * 1024
        ),
    )(sources, turned, validity, *tables)


def solution(mesh):
    chans = mesh.shape["chan"]
    length = 7680
    tables = constant_tables(length, chans)
    return jax.shard_map(
        functools.partial(local, tables),
        mesh=mesh,
        in_specs=(P("seg", None, "chan"), P(), P()),
        out_specs=P("seg", "chan", None),
        check_vma=False,
    )
```

```python
import functools
import math

import jax
import jax.numpy as jnp
import numpy as np
from jax import lax
from jax.experimental import pallas as pl
from jax.experimental.pallas import tpu as pltpu
from jax.sharding import PartitionSpec as P

LAGS = 512
EPSILON = 1e-06
MESH = pl.DeviceIdType.MESH
CHUNKS = 8
STEPS = 32000.0
F32 = jnp.float32
BF16 = jnp.bfloat16


def constant_tables(length, blocks):
    block_len = length // blocks
    half = block_len // 2
    q = np.arange(block_len)[:, None]
    k1 = np.arange(blocks)[:, None]
    k2 = np.arange(half)[None, :]
    angle = 2.0 * math.pi / length * ((k1 * q.T) % length)
    twist = np.zeros((2, blocks, 512), np.float32)
    twist[0, :, :block_len] = np.cos(angle)
    twist[1, :, :block_len] = np.sin(angle)
    angle = 2.0 * math.pi / block_len * ((q * k2) % block_len)
    second = np.zeros((2, 512, 256), np.float32)
    second[0, :block_len, :half] = np.cos(angle)
    second[1, :block_len, :half] = np.sin(angle)
    second_hi = second.astype(jnp.bfloat16)
    second_lo = (second - second_hi.astype(np.float32)).astype(jnp.bfloat16)
    lag = (np.arange(LAGS) - LAGS // 2)[None, :]
    angle = 2.0 * math.pi / length * ((k1 * lag) % length)
    lag_one = np.stack([np.cos(angle), np.sin(angle)]).astype(np.float32)
    angle = 2.0 * math.pi / block_len * ((k2.T * lag) % block_len)
    lag_two = np.zeros((2, 256, LAGS), np.float32)
    lag_two[0, :half] = 2.0 * np.cos(angle)
    lag_two[1, :half] = 2.0 * np.sin(angle)
    return twist, second_hi, second_lo, lag_one, lag_two


def times_root(value, k, n):
    re, im = value
    c, s = math.cos(2.0 * math.pi * k / n), math.sin(2.0 * math.pi * k / n)
    if k == 0:
        return value
    if 4 * k == n:
        return (im, -re)
    if 2 * k == n:
        return (-re, None if im is None else -im)
    if im is None:
        return (re * c, re * (-s))
    return (re * c + im * s, im * c - re * s)


def plus(a, b):
    if a is None:
        return b
    return a if b is None else a + b


def conj(value):
    re, im = value
    return (re, None if im is None else -im)


def real_dft(xs):
    n = len(xs)
    if n == 2:
        return [(xs[0] + xs[1], None), (xs[0] - xs[1], None)]
    even, odd = real_dft(xs[0::2]), real_dft(xs[1::2])
    h = n // 2
    out = []
    for k in range(h + 1):
        i = k % h
        e = even[i] if i <= h // 2 else conj(even[h - i])
        o = odd[i] if i <= h // 2 else conj(odd[h - i])
        t = times_root(o, k, n)
        out.append((plus(e[0], t[0]), plus(e[1], t[1])))
    return out


def split(value):
    hi = value.astype(BF16)
    return hi, (value - hi.astype(F32)).astype(BF16)


def dot(a, b):
    return jnp.dot(a, b, preferred_element_type=F32)


def body(
    sources,
    traces,
    validity,
    twist_in,
    second_hi,
    second_lo,
    lag_one,
    lag_two,
    out,
    names_smem,
    staged,
    valid_in,
    twist,
    sec_hi,
    sec_lo,
    one,
    two,
    own_send,
    src_send,
    own_recv,
    src_recv,
    h_hi,
    h_lo,
    table_hi,
    table_lo,
    spec,
    white,
    white_send,
    white_recv,
    gathered,
    lag_table,
    prod_a,
    prod_b,
    acc,
    part_send,
    part_recv,
    in_sem,
    own_ss,
    own_rs,
    src_ss,
    src_rs,
    ag_ss,
    fw_ss,
    ag_rs,
    wh_ss,
    wh_rs,
    rs_ss,
    rs_rs,
):
    chans = lax.axis_size("chan")
    segs = lax.axis_size("seg")
    me = lax.axis_index("chan")
    seg = lax.axis_index("seg")
    chip = me // 2
    core = me % 2
    z = chip // 2
    plane = chip % 2
    zs = chans // 4
    block_len = traces.shape[1]
    partner = (2 * chip + 1 - core, seg)

    def iota(shape, axis):
        return lax.broadcasted_iota(jnp.int32, shape, axis)

    def remote(src, dst, send, recv, to):
        return pltpu.make_async_remote_copy(
            src_ref=src,
            dst_ref=dst,
            send_sem=send,
            recv_sem=recv,
            device_id=to,
            device_id_type=MESH,
        )

    def device(zz, pp, cc):
        return (zz % zs) * 4 + pp * 2 + cc

    def octet_of(zz, pp):
        return 2 * zz + (zz + pp) % 2

    barrier = pltpu.get_barrier_semaphore()
    for d in sorted(range(1, chans), key=lambda d: abs(d - chans // 2)):
        pl.semaphore_signal(
            barrier, inc=1, device_id=((me + d) % chans, seg), device_id_type=MESH
        )
    for d in range(1, segs):
        for p in range(2):
            pl.semaphore_signal(
                barrier,
                inc=1,
                device_id=(device(z, p, core), (seg + d) % segs),
                device_id_type=MESH,
            )

    fetch = [
        pltpu.make_async_copy(a, b, in_sem.at[n])
        for n, (a, b) in enumerate(
            [(traces.at[g], staged.at[g]) for g in range(4)]
            + [
                (sources, names_smem),
                (validity, valid_in),
                (twist_in, twist),
                (second_hi, sec_hi),
                (second_lo, sec_lo),
                (lag_one, one),
                (lag_two, two),
            ]
        )
    ]
    for n in (4, 0, 1, 2, 3, 7, 8, 9, 10, 5, 6):
        fetch[n].start()

    fetch[4].wait()
    all_chans = staged.shape[2]
    count = 8 * chans // 2
    names = jnp.zeros((count, 1), jnp.int32)
    r_names = iota((count, 1), 0)
    for s in range(count):
        names = jnp.where(r_names == s, names_smem[s], names)
    row = iota((all_chans, 1), 0)
    pick = jnp.concatenate([row, names], 0)
    pick = (iota((all_chans + count, all_chans), 1) == pick).astype(F32).astype(BF16)

    def steps_of(g):
        fetch[g].wait()
        x = staged[g]
        top = jnp.maximum(jnp.max(jnp.abs(x), axis=0, keepdims=True), 1e-30)
        power = jnp.ceil(jnp.log(top) * (128.0 / math.log(2.0))) + 1.0
        steps = jnp.round(x * (STEPS / jnp.exp2(power * (1.0 / 128.0))))
        tail = jnp.where(iota((512 - block_len, all_chans), 0) == 0, power, 0.0)
        steps = jnp.concatenate([steps, tail], 0)
        high = jnp.round(steps * (1.0 / 256.0))
        low = steps - 256.0 * high
        dims = (((1,), (1,)), ((), ()))
        return 256.0 * lax.dot_general(
            pick, high.astype(BF16), dims, preferred_element_type=F32
        ) + lax.dot_general(pick, low.astype(BF16), dims, preferred_element_type=F32)

    for i in range(2):
        pair = [steps_of(2 * i + gg).reshape(-1, 8, 512) for gg in range(2)]
        both = jnp.concatenate(pair, axis=1).astype(jnp.int32).astype(jnp.int16)
        own_send[i] = both[:chans]
        src_send[i] = both[chans:]

    pl.semaphore_wait(barrier, chans - 1 + 2 * (segs - 1))

    src_copies, own_copies = [], [[], []]
    for d in range(1, chans):
        to = (me + d) % chans
        copy = remote(
            src_send.at[to % 2, octet_of(to // 4, (to // 2) % 2)],
            src_recv.at[me],
            src_ss.at[d],
            src_rs.at[d],
            (to, seg),
        )
        copy.start()
        src_copies.append(copy)
    for i in range(2):
        for d in range(1, chans):
            to = (me + d) % chans
            copy = remote(
                own_send.at[i, to],
                own_recv.at[i, me],
                own_ss.at[i, d],
                own_rs.at[i, d],
                (to, seg),
            )
            copy.start()
            own_copies[i].append(copy)
    src_recv[pl.ds(me, 1)] = src_send[core, pl.ds(octet_of(z, plane), 1)]
    for i in range(2):
        own_recv[i, pl.ds(me, 1)] = own_send[i, pl.ds(me, 1)]

    for n in range(5, 11):
        fetch[n].wait()

    table_hi[:512, :256] = sec_hi[0]
    table_hi[512:, :256] = sec_hi[1]
    table_hi[:512, 256:] = -sec_hi[1]
    table_hi[512:, 256:] = sec_hi[0]
    table_lo[:512, :256] = sec_lo[0]
    table_lo[512:, :256] = sec_lo[1]
    table_lo[:512, 256:] = -sec_lo[1]
    table_lo[512:, 256:] = sec_lo[0]

    def fill(k1, carry):
        c1 = one[0, pl.ds(k1, 1), :]
        s1 = one[1, pl.ds(k1, 1), :]

        def rows(i, inner):
            r = pl.multiple_of(i * 16, 16)
            c2 = two[0, pl.ds(r, 16), :]
            s2 = two[1, pl.ds(r, 16), :]
            c = c1 * c2 - s1 * s2
            s = s1 * c2 + c1 * s2
            lag_table[k1, pl.ds(r, 16), :] = (c - s).astype(BF16)
            lag_table[k1, pl.ds(r + 256, 16), :] = s.astype(BF16)
            lag_table[k1, pl.ds(r + 512, 16), :] = (-c).astype(BF16)
            return inner

        return lax.fori_loop(0, 16, rows, carry)

    lax.fori_loop(0, chans, fill, 0)
    first = iota((16, LAGS), 0) == 0
    for r in (0, 256, 512):
        head = lag_table[0, r : r + 16, :].astype(F32)
        lag_table[0, r : r + 16, :] = jnp.where(first, 0.5 * head, head).astype(BF16)

    valid = valid_in[...].astype(F32).astype(BF16)
    all_segs = valid.shape[0]

    def gate_of(row_seg, row_chan, rows):
        seg_hot = (iota((rows, all_segs), 1) == row_seg).astype(F32).astype(BF16)
        chan_hot = (iota((rows, all_chans), 1) == row_chan).astype(F32)
        return jnp.sum(dot(seg_hot, valid) * chan_hot, axis=1, keepdims=True)

    def named(r, base):
        found = jnp.zeros(r.shape, jnp.int32)
        for s in range(8):
            found = jnp.where(r == s, names_smem[8 * base + s], found)
        return found

    r16 = iota((16, 1), 0)
    own_gates = [
        gate_of(4 * seg + 2 * i + r16 // 8, 8 * me + r16 % 8, 16) for i in range(2)
    ]
    src_gate = gate_of(4 * seg + 2 * core + r16 // 8, named(r16 % 8, octet_of(z, plane)), 16)
    want = iota((8, all_chans), 1) == named(iota((8, 1), 0), seg)
    want_valid = lax.dot_general(
        want.astype(F32).astype(BF16),
        valid,
        (((1,), (1,)), ((), ())),
        preferred_element_type=F32,
    ).astype(BF16)
    pairs_all = dot(want_valid, valid)
    shift_hot = (iota((all_chans, 128), 0) == 8 * me + iota((all_chans, 128), 1)).astype(F32)
    pairs = dot(pairs_all.astype(BF16), shift_hot.astype(BF16))
    bins_total = chans * block_len // 2
    scale = 1.0 / jnp.sqrt(2.0 * bins_total * jnp.maximum(pairs, 1.0))

    spread = (iota((256, 256), 0) // 8 == iota((256, 256), 1) // 8).astype(F32).astype(BF16)

    def transform(recv, gate, store):
        units = []
        for p in range(chans):
            last = recv[p, :, 384:512].astype(jnp.int32).astype(F32)
            at = block_len - 384
            units.append(jnp.exp2(last[:, at : at + 1] * (1.0 / 128.0)) * (1.0 / STEPS))
        for a in range(0, 512, 128):
            xs = [
                recv[p, :, a : a + 128].astype(jnp.int32).astype(F32) * units[p]
                for p in range(chans)
            ]
            half = real_dft(xs)
            for k in range(chans):
                g = half[k] if k <= chans // 2 else conj(half[chans - k])
                re, im = g
                c = twist[0, k : k + 1, a : a + 128]
                s = twist[1, k : k + 1, a : a + 128]
                if im is None:
                    re, im = re * c, -(re * s)
                else:
                    re, im = re * c + im * s, im * c - re * s
                at = slice(16 * k, 16 * k + 16)
                hi, lo = split(re)
                h_hi[at, a : a + 128] = hi
                h_lo[at, a : a + 128] = lo
                hi, lo = split(im)
                h_hi[at, 512 + a : 640 + a] = hi
                h_lo[at, 512 + a : 640 + a] = lo
        spec[...] = (
            dot(h_hi[...], table_hi[...])
            + dot(h_lo[...], table_hi[...])
            + dot(h_hi[...], table_lo[...])
        )
        total = None
        for k in range(chans):
            re, im = spec[16 * k : 16 * k + 16, :256], spec[16 * k : 16 * k + 16, 256:]
            total = plus(total, jnp.sqrt(re * re + im * im))
        hi, lo = split(total)
        mean = (dot(hi, spread) + dot(lo, spread)) * (1.0 / 128.0) + EPSILON
        factor = gate / mean
        for k in range(chans):
            for part in range(2):
                at = slice(256 * part, 256 * part + 256)
                store(k, at, (spec[16 * k : 16 * k + 16, at] * factor).astype(BF16))

    per = chans // CHUNKS
    slot = 2 * z + core

    def span(ch):
        return pl.ds(ch * per, per)

    def store_src(k, at, value):
        gathered[slot, k, :, at] = value

    for copy in src_copies:
        copy.wait_recv()
    transform(src_recv, src_gate, store_src)

    def gather(ch, d):
        ref = gathered.at[slot, span(ch)]
        to = partner if d == 0 else (device(z + d, plane, core), seg)
        return remote(ref, ref, ag_ss.at[ch, d], ag_rs.at[ch, slot], to)

    def slot_of(d, cc):
        return 2 * ((z + d) % zs) + cc

    def forward(ch, d):
        at = slot_of(d, core)
        ref = gathered.at[at, span(ch)]
        return remote(ref, ref, fw_ss.at[ch, d], ag_rs.at[ch, at], partner)

    def arrive(ch, d, cc):
        at = slot_of(d, cc)
        ref = gathered.at[at, span(ch)]
        remote(ref, ref, fw_ss.at[ch, 0], ag_rs.at[ch, at], partner).wait_recv()

    for ch in range(CHUNKS):
        for d in range(zs - 1, -1, -1):
            gather(ch, d).start()

    rest = [(1, ch) for ch in range(CHUNKS)]
    for ch in range(3, CHUNKS):
        rest.insert(2 * ch - 3, (0, ch))
    across = (device(z, 1 - plane, core), seg)

    def cross(i, ch):
        return remote(
            white_send.at[i, span(ch)],
            white_recv.at[i, span(ch)],
            wh_ss.at[i, ch],
            wh_rs.at[i, ch],
            across,
        )

    for i in range(2):

        def store_own(k, at, value, i=i):
            white_send[i, k, :, at] = value
            white[plane, k, 16 * i : 16 * i + 16, at] = value.astype(F32)

        for copy in own_copies[i]:
            copy.wait_recv()
        transform(own_recv.at[i], own_gates[i], store_own)
        for pair in [(0, ch) for ch in range(3)] if i == 0 else rest:
            cross(*pair).start()

    acc[...] = jnp.zeros_like(acc)
    prod_b[...] = jnp.zeros_like(prod_b)

    def stack(k, half, prod):
        for l in range(2):
            re_at, im_at = l * 128, 256 + l * 128
            ar, ap, am = [], [], []
            for oo in range(2):
                for h in range(2):
                    slot_at = 2 * (2 * half + oo) + h
                    re = gathered[slot_at, k, :, re_at : re_at + 128].astype(F32)
                    im = gathered[slot_at, k, :, im_at : im_at + 128].astype(F32)
                    for part in (slice(0, 8), slice(8, 16)):
                        ar.append(re[part])
                        ap.append(re[part] + im[part])
                        am.append(re[part] - im[part])
            for c in range(0, 16, 2):
                rows = [[[], [], []], [[], [], []]]
                for cc in (c, c + 1):
                    sums = [[None] * 3, [None] * 3]
                    for g in range(4):
                        at = 8 * g + cc % 8
                        br = white[cc // 8, k, at : at + 1, re_at : re_at + 128]
                        bi = white[cc // 8, k, at : at + 1, im_at : im_at + 128]
                        bs = br + bi
                        for oo in range(2):
                            n = 4 * oo + g
                            sums[oo] = [
                                plus(sums[oo][0], ar[n] * bs),
                                plus(sums[oo][1], ap[n] * br),
                                plus(sums[oo][2], am[n] * bi),
                            ]
                    for oo in range(2):
                        for m in range(3):
                            rows[oo][m].append(sums[oo][m])
                for oo in range(2):
                    at = 256 * half + 128 * oo + 8 * c
                    for m in range(3):
                        lane = 256 * m + 128 * l
                        prod[at : at + 16, lane : lane + 128] = jnp.concatenate(
                            rows[oo][m], 0
                        ).astype(BF16)

    def relay(ch):
        for d in range(1, zs):
            arrive(ch, d, core)
            forward(ch, d).start()

    def ready(ch):
        for d in range(zs):
            arrive(ch, d, 1 - core)
        for i in range(2):
            cross(i, ch).wait_recv()
            for j in range(per):
                k = ch * per + j
                white[1 - plane, k, 16 * i : 16 * i + 16, :] = white_recv[i, k].astype(F32)

    bufs = [prod_a, prod_b]

    def chunk(ch, carry):
        relay(ch + 1)
        ready(ch)
        for j in range(per):
            k = ch * per + j
            acc[...] += dot(bufs[1 - j % 2][...], lag_table[jnp.maximum(k - 1, 0)])
            stack(k, 0, bufs[j % 2])
            stack(k, 1, bufs[j % 2])
        return carry

    relay(0)
    lax.fori_loop(0, CHUNKS - 1, chunk, 0)

    def partial(o, p):
        rows = part_send.at[128 * o + 64 * p : 128 * o + 64 * p + 64]
        to = (device(z, p, core), octet_of(o, plane))
        return remote(rows, part_recv.at[seg], rs_ss.at[o, p], rs_rs.at[seg], to)

    def remains(o, p):
        return jnp.logical_and(plane == p, seg == octet_of(o, plane))

    def scatter(half):
        part_send[256 * half : 256 * half + 256] = acc[256 * half : 256 * half + 256].astype(BF16)
        for o in (2 * half, 2 * half + 1):
            for p in range(2):

                @pl.when(jnp.logical_not(remains(o, p)))
                def _(o=o, p=p):
                    partial(o, p).start()

                @pl.when(remains(o, p))
                def _(o=o, p=p):
                    part_recv[pl.ds(seg, 1)] = part_send[
                        128 * o + 64 * p : 128 * o + 64 * p + 64
                    ][None]

    ready(CHUNKS - 1)
    last = chans - per

    def lags(half, k, prod):
        at = slice(256 * half, 256 * half + 256)
        acc[at] += dot(prod[at, :], lag_table[k])

    stack(last, 0, prod_a)
    for half in range(2):
        lags(half, last - 1, prod_b)
    stack(last + 1, 0, prod_b)
    lags(0, last, prod_a)
    stack(last, 1, prod_a)
    lags(0, last + 1, prod_b)
    scatter(0)
    stack(last + 1, 1, prod_b)
    lags(1, last, prod_a)
    lags(1, last + 1, prod_b)
    scatter(1)

    for copy in src_copies + own_copies[0] + own_copies[1]:
        copy.wait_send()
    for ch in range(CHUNKS):
        for d in range(zs):
            gather(ch, d).wait_send()
        for d in range(1, zs):
            forward(ch, d).wait_send()
        for i in range(2):
            cross(i, ch).wait_send()
    def landed(d):
        at = (seg + d) % segs
        ref = part_recv.at[at]
        remote(ref, ref, rs_ss.at[0, 0], rs_rs.at[at], partner).wait_recv()

    @pl.when((seg + seg // 2) % 2 != plane)
    def _():
        landed(0)

    for d in range(1, segs):
        landed(d)
    for c in range(8):
        total = part_recv[0, 8 * c : 8 * c + 8, :].astype(F32)
        for j in range(1, segs):
            total += part_recv[j, 8 * c : 8 * c + 8, :].astype(F32)
        out[:, c, :] = total * scale[:, c : c + 1]

    for o in range(zs):
        for p in range(2):

            @pl.when(jnp.logical_not(remains(o, p)))
            def _(o=o, p=p):
                partial(o, p).wait_send()


def local(tables, traces, sources, validity):
    chans = lax.axis_size("chan")
    segs = lax.axis_size("seg")
    vmem = pl.BlockSpec(memory_space=pltpu.VMEM)
    hbm = pl.BlockSpec(memory_space=pl.ANY)
    dma = pltpu.SemaphoreType.DMA
    turned = traces.transpose(0, 2, 1)
    tables = [jnp.asarray(t) for t in tables]
    return pl.pallas_call(
        body,
        name="correlate",
        out_shape=jax.ShapeDtypeStruct((8, 8, LAGS), F32),
        in_specs=[hbm] * 8,
        out_specs=vmem,
        scratch_shapes=[
            pltpu.SMEM(sources.shape, jnp.int32),
            pltpu.VMEM(turned.shape, F32),
            pltpu.VMEM(validity.shape, jnp.int32),
            *[pltpu.VMEM(t.shape, t.dtype) for t in tables],
            pltpu.VMEM((2, chans, 16, 512), jnp.int16),
            pltpu.VMEM((2, chans // 2, 16, 512), jnp.int16),
            pltpu.VMEM((2, chans, 16, 512), jnp.int16),
            pltpu.VMEM((chans, 16, 512), jnp.int16),
            pltpu.VMEM((16 * chans, 1024), BF16),
            pltpu.VMEM((16 * chans, 1024), BF16),
            pltpu.VMEM((1024, 512), BF16),
            pltpu.VMEM((1024, 512), BF16),
            pltpu.VMEM((16 * chans, 512), F32),
            pltpu.VMEM((2, chans, 32, 512), F32),
            pltpu.VMEM((2, chans, 16, 512), BF16),
            pltpu.VMEM((2, chans, 16, 512), BF16),
            pltpu.VMEM((8, chans, 16, 512), BF16),
            pltpu.VMEM((chans, 768, LAGS), BF16),
            pltpu.VMEM((512, 768), BF16),
            pltpu.VMEM((512, 768), BF16),
            pltpu.VMEM((512, LAGS), F32),
            pltpu.VMEM((512, LAGS), BF16),
            pltpu.VMEM((segs, 64, LAGS), BF16),
            dma((11,)),
            dma((2, chans)),
            dma((2, chans)),
            dma((chans,)),
            dma((chans,)),
            dma((CHUNKS, 4)),
            dma((CHUNKS, 4)),
            dma((CHUNKS, 8)),
            dma((2, CHUNKS)),
            dma((2, CHUNKS)),
            dma((4, 2)),
            dma((segs,)),
        ],
        compiler_params=pltpu.CompilerParams(
            collective_id=0, has_side_effects=True, vmem_limit_bytes=60 * 1024 * 1024
        ),
    )(sources, turned, validity, *tables)


def solution(mesh):
    chans = mesh.shape["chan"]
    length = 7680
    tables = constant_tables(length, chans)
    return jax.shard_map(
        functools.partial(local, tables),
        mesh=mesh,
        in_specs=(P("seg", None, "chan"), P(), P()),
        out_specs=P("seg", "chan", None),
        check_vma=False,
    )
```

```python
import functools
import math

import jax
import jax.numpy as jnp
import numpy as np
from jax import lax
from jax.experimental import pallas as pl
from jax.experimental.pallas import tpu as pltpu
from jax.sharding import PartitionSpec as P

LAGS = 512
EPSILON = 1e-06
MESH = pl.DeviceIdType.MESH
CHUNKS = 8
STEPS = 32000.0
F32 = jnp.float32
BF16 = jnp.bfloat16


def constant_tables(length, blocks):
    block_len = length // blocks
    half = block_len // 2
    q = np.arange(block_len)[:, None]
    k1 = np.arange(blocks)[:, None]
    k2 = np.arange(half)[None, :]
    angle = 2.0 * math.pi / length * ((k1 * q.T) % length)
    twist = np.zeros((2, blocks, 512), np.float32)
    twist[0, :, :block_len] = np.cos(angle)
    twist[1, :, :block_len] = np.sin(angle)
    angle = 2.0 * math.pi / block_len * ((q * k2) % block_len)
    second = np.zeros((2, 512, 256), np.float32)
    second[0, :block_len, :half] = np.cos(angle)
    second[1, :block_len, :half] = np.sin(angle)
    second_hi = second.astype(jnp.bfloat16)
    second_lo = (second - second_hi.astype(np.float32)).astype(jnp.bfloat16)
    lag = (np.arange(LAGS) - LAGS // 2)[None, :]
    angle = 2.0 * math.pi / length * ((k1 * lag) % length)
    lag_one = np.stack([np.cos(angle), np.sin(angle)]).astype(np.float32)
    angle = 2.0 * math.pi / block_len * ((k2.T * lag) % block_len)
    lag_two = np.zeros((2, 256, LAGS), np.float32)
    lag_two[0, :half] = 2.0 * np.cos(angle)
    lag_two[1, :half] = 2.0 * np.sin(angle)
    return twist, second_hi, second_lo, lag_one, lag_two


def times_root(value, k, n):
    re, im = value
    c, s = math.cos(2.0 * math.pi * k / n), math.sin(2.0 * math.pi * k / n)
    if k == 0:
        return value
    if 4 * k == n:
        return (im, -re)
    if 2 * k == n:
        return (-re, None if im is None else -im)
    if im is None:
        return (re * c, re * (-s))
    return (re * c + im * s, im * c - re * s)


def plus(a, b):
    if a is None:
        return b
    return a if b is None else a + b


def conj(value):
    re, im = value
    return (re, None if im is None else -im)


def real_dft(xs):
    n = len(xs)
    if n == 2:
        return [(xs[0] + xs[1], None), (xs[0] - xs[1], None)]
    even, odd = real_dft(xs[0::2]), real_dft(xs[1::2])
    h = n // 2
    out = []
    for k in range(h + 1):
        i = k % h
        e = even[i] if i <= h // 2 else conj(even[h - i])
        o = odd[i] if i <= h // 2 else conj(odd[h - i])
        t = times_root(o, k, n)
        out.append((plus(e[0], t[0]), plus(e[1], t[1])))
    return out


def split(value):
    hi = value.astype(BF16)
    return hi, (value - hi.astype(F32)).astype(BF16)


def dot(a, b):
    return jnp.dot(a, b, preferred_element_type=F32)


def body(
    sources,
    traces,
    validity,
    twist_in,
    second_hi,
    second_lo,
    lag_one,
    lag_two,
    out,
    names_smem,
    staged,
    valid_in,
    twist,
    sec_hi,
    sec_lo,
    one,
    two,
    own_send,
    src_send,
    own_recv,
    src_recv,
    hi_a,
    hi_b,
    lo_a,
    lo_b,
    table_hi,
    table_lo,
    spec,
    white,
    white_send,
    white_recv,
    gathered,
    lag_table,
    prod_a,
    prod_b,
    acc,
    part_send,
    part_recv,
    in_sem,
    own_ss,
    own_rs,
    src_sem,
    ag_ss,
    ag_rs,
    wh_ss,
    wh_rs,
    rs_ss,
    rs_rs,
):
    chans = lax.axis_size("chan")
    segs = lax.axis_size("seg")
    me = lax.axis_index("chan")
    seg = lax.axis_index("seg")
    chip, core = lax.div(me, 2), lax.rem(me, 2)
    z, plane = lax.div(chip, 2), lax.rem(chip, 2)
    zs = chans // 4
    block_len = traces.shape[1]
    partner = (2 * chip + 1 - core, seg)

    def iota(shape, axis):
        return lax.broadcasted_iota(jnp.int32, shape, axis)

    def remote(src, dst, send, recv, to):
        return pltpu.make_async_remote_copy(
            src_ref=src,
            dst_ref=dst,
            send_sem=send,
            recv_sem=recv,
            device_id=to,
            device_id_type=MESH,
        )

    def device(zz, pp, cc):
        return lax.rem(zz, zs) * 4 + pp * 2 + cc

    def octet_of(zz, pp):
        return 2 * zz + lax.rem(zz + pp, 2)

    barrier = pltpu.get_barrier_semaphore()
    for d in sorted(range(1, chans), key=lambda d: abs(d - chans // 2)):
        pl.semaphore_signal(
            barrier, inc=1, device_id=(lax.rem(me + d, chans), seg), device_id_type=MESH
        )
    for d in range(1, segs):
        for p in range(2):
            pl.semaphore_signal(
                barrier,
                inc=1,
                device_id=(device(z, p, core), lax.rem(seg + d, segs)),
                device_id_type=MESH,
            )

    fetch = [
        pltpu.make_async_copy(a, b, in_sem.at[n])
        for n, (a, b) in enumerate(
            [(traces.at[g], staged.at[g]) for g in range(4)]
            + [
                (sources, names_smem),
                (validity, valid_in),
                (twist_in, twist),
                (second_hi, sec_hi),
                (second_lo, sec_lo),
                (lag_one, one),
                (lag_two, two),
            ]
        )
    ]
    for n in (4, 0, 1, 2, 3, 7, 8, 9, 10, 5, 6):
        fetch[n].start()

    fetch[4].wait()
    all_chans = staged.shape[2]
    count = 8 * chans // 2
    names = jnp.zeros((count, 1), jnp.int32)
    r_names = iota((count, 1), 0)
    for s in range(count):
        names = jnp.where(r_names == s, names_smem[s], names)
    row = iota((all_chans, 1), 0)
    pick = jnp.concatenate([row, names], 0)
    pick = (iota((all_chans + count, all_chans), 1) == pick).astype(F32).astype(BF16)

    def steps_of(g):
        fetch[g].wait()
        x = staged[g]
        top = jnp.maximum(jnp.max(jnp.abs(x), axis=0, keepdims=True), 1e-30)
        power = jnp.ceil(jnp.log(top) * (128.0 / math.log(2.0))) + 1.0
        steps = jnp.round(x * (STEPS / jnp.exp2(power * (1.0 / 128.0))))
        tail = jnp.where(iota((512 - block_len, all_chans), 0) == 0, power, 0.0)
        steps = jnp.concatenate([steps, tail], 0)
        high = jnp.round(steps * (1.0 / 256.0))
        low = steps - 256.0 * high
        dims = (((1,), (1,)), ((), ()))
        return 256.0 * lax.dot_general(
            pick, high.astype(BF16), dims, preferred_element_type=F32
        ) + lax.dot_general(pick, low.astype(BF16), dims, preferred_element_type=F32)

    for i in range(2):
        pair = [steps_of(2 * i + gg).reshape(-1, 8, 512) for gg in range(2)]
        both = jnp.concatenate(pair, axis=1).astype(jnp.int32).astype(jnp.int16)
        own_send[i] = both[:chans]
        src_send[i] = both[chans:]

    pl.semaphore_wait(barrier, chans - 1 + 2 * (segs - 1))

    others = pl.ds(0, chans - 1)
    for d in range(1, chans):
        to = lax.rem(me + d, chans)
        remote(
            src_send.at[lax.rem(to, 2), octet_of(lax.div(to, 4), lax.rem(lax.div(to, 2), 2))],
            src_recv.at[me],
            src_sem.at[0],
            src_sem.at[1],
            (to, seg),
        ).start()
    for i in range(2):
        for d in range(1, chans):
            to = lax.rem(me + d, chans)
            remote(
                own_send.at[i, to], own_recv.at[i, me], own_ss.at[i], own_rs.at[i], (to, seg)
            ).start()

    def all_sources():
        ref = src_recv.at[others]
        return remote(ref, ref, src_sem.at[0], src_sem.at[1], partner)

    def all_own(i):
        ref = own_recv.at[i, others]
        return remote(ref, ref, own_ss.at[i], own_rs.at[i], partner)

    src_recv[pl.ds(me, 1)] = src_send[core, pl.ds(octet_of(z, plane), 1)]
    for i in range(2):
        own_recv[i, pl.ds(me, 1)] = own_send[i, pl.ds(me, 1)]

    for n in range(5, 11):
        fetch[n].wait()

    for table, sec in ((table_hi, sec_hi), (table_lo, sec_lo)):
        for n in range(2):
            at, low = slice(256 * n, 256 * n + 256), 512 * n
            table[low : low + 256, :256] = sec[0, at]
            table[low : low + 256, 256:] = -sec[1, at]
            table[low + 256 : low + 512, :256] = sec[1, at]
            table[low + 256 : low + 512, 256:] = sec[0, at]

    def fill(k1, carry):
        c1 = one[0, pl.ds(k1, 1), :]
        s1 = one[1, pl.ds(k1, 1), :]

        def rows(i, inner):
            r = pl.multiple_of(i * 16, 16)
            c2 = two[0, pl.ds(r, 16), :]
            s2 = two[1, pl.ds(r, 16), :]
            c = c1 * c2 - s1 * s2
            s = s1 * c2 + c1 * s2
            lag_table[k1, pl.ds(r, 16), :] = (c - s).astype(BF16)
            lag_table[k1, pl.ds(r + 256, 16), :] = s.astype(BF16)
            lag_table[k1, pl.ds(r + 512, 16), :] = (-c).astype(BF16)
            return inner

        return lax.fori_loop(0, 16, rows, carry)

    lax.fori_loop(0, chans, fill, 0)
    first = iota((16, LAGS), 0) == 0
    for r in (0, 256, 512):
        head = lag_table[0, r : r + 16, :].astype(F32)
        lag_table[0, r : r + 16, :] = jnp.where(first, 0.5 * head, head).astype(BF16)

    valid = valid_in[...].astype(F32).astype(BF16)
    all_segs = valid.shape[0]

    def gate_of(row_seg, row_chan, rows):
        seg_hot = (iota((rows, all_segs), 1) == row_seg).astype(F32).astype(BF16)
        chan_hot = (iota((rows, all_chans), 1) == row_chan).astype(F32)
        return jnp.sum(dot(seg_hot, valid) * chan_hot, axis=1, keepdims=True)

    def named(r, base):
        found = jnp.zeros(r.shape, jnp.int32)
        for s in range(8):
            found = jnp.where(r == s, names_smem[8 * base + s], found)
        return found

    r16 = iota((16, 1), 0)
    own_gates = [
        gate_of(4 * seg + 2 * i + r16 // 8, 8 * me + r16 % 8, 16) for i in range(2)
    ]
    src_gate = gate_of(4 * seg + 2 * core + r16 // 8, named(r16 % 8, octet_of(z, plane)), 16)
    want = iota((8, all_chans), 1) == named(iota((8, 1), 0), seg)
    want_valid = lax.dot_general(
        want.astype(F32).astype(BF16),
        valid,
        (((1,), (1,)), ((), ())),
        preferred_element_type=F32,
    ).astype(BF16)
    pairs_all = dot(want_valid, valid)
    shift_hot = (iota((all_chans, 128), 0) == 8 * me + iota((all_chans, 128), 1)).astype(F32)
    pairs = dot(pairs_all.astype(BF16), shift_hot.astype(BF16))
    bins_total = chans * block_len // 2
    scale = 1.0 / jnp.sqrt(2.0 * bins_total * jnp.maximum(pairs, 1.0))

    spread = (iota((256, 256), 0) // 8 == iota((256, 256), 1) // 8).astype(F32).astype(BF16)

    def half_dot(hi, lo, low):
        at = slice(low, low + 512)
        return (
            dot(hi[...], table_hi[at]) + dot(lo[...], table_hi[at]) + dot(hi[...], table_lo[at])
        )

    def transform(recv, gate, store):
        units = []
        for p in range(chans):
            last = recv[p, :, 384:512].astype(jnp.int32).astype(F32)
            at = block_len - 384
            units.append(jnp.exp2(last[:, at : at + 1] * (1.0 / 128.0)) * (1.0 / STEPS))
        for a in range(0, 512, 128):
            h_hi, h_lo = (hi_a, lo_a) if a < 256 else (hi_b, lo_b)
            xs = [
                recv[p, :, a : a + 128].astype(jnp.int32).astype(F32) * units[p]
                for p in range(chans)
            ]
            half = real_dft(xs)
            for k in range(chans):
                g = half[k] if k <= chans // 2 else conj(half[chans - k])
                re, im = g
                c = twist[0, k : k + 1, a : a + 128]
                s = twist[1, k : k + 1, a : a + 128]
                if im is None:
                    re, im = re * c, -(re * s)
                else:
                    re, im = re * c + im * s, im * c - re * s
                at = slice(16 * k, 16 * k + 16)
                hi, lo = split(re)
                b = a % 256
                h_hi[at, b : b + 128] = hi
                h_lo[at, b : b + 128] = lo
                hi, lo = split(im)
                h_hi[at, 256 + b : 384 + b] = hi
                h_lo[at, 256 + b : 384 + b] = lo
            if a == 128:
                spec[...] = half_dot(hi_a, lo_a, 0)
        spec[...] += half_dot(hi_b, lo_b, 512)
        total = None
        for k in range(chans):
            re, im = spec[16 * k : 16 * k + 16, :256], spec[16 * k : 16 * k + 16, 256:]
            total = plus(total, jnp.sqrt(re * re + im * im))
        hi, lo = split(total)
        mean = (dot(hi, spread) + dot(lo, spread)) * (1.0 / 128.0) + EPSILON
        factor = gate / mean
        for k in range(chans):
            for part in range(2):
                at = slice(256 * part, 256 * part + 256)
                store(k, at, (spec[16 * k : 16 * k + 16, at] * factor).astype(BF16))

    per = chans // CHUNKS
    slot = 2 * z + core

    def span(ch):
        return pl.ds(ch * per, per)

    def store_src(k, at, value):
        gathered[slot, k, :, at] = value

    all_sources().wait_recv()
    transform(src_recv, src_gate, store_src)

    def gather(ch, d):
        ref = gathered.at[slot, span(ch)]
        to = partner if d == 0 else (device(z + d, plane, core), seg)
        return remote(ref, ref, ag_ss.at[0], ag_rs.at[ch, int(d == 0)], to)

    def slot_of(d, cc):
        return 2 * lax.rem(z + d, zs) + cc

    def forward(ch, d):
        at = slot_of(d, core)
        ref = gathered.at[at, span(ch)]
        return remote(ref, ref, ag_ss.at[1], ag_rs.at[ch, 1], partner)

    def arrive(ch, way, blocks):
        ref = gathered.at[pl.ds(0, blocks), span(ch)]
        remote(ref, ref, ag_ss.at[0], ag_rs.at[ch, way], partner).wait_recv()

    for ch in range(CHUNKS):
        for d in range(zs - 1, -1, -1):
            gather(ch, d).start()

    rest = [(1, ch) for ch in range(CHUNKS)]
    for ch in range(3, CHUNKS):
        rest.insert(2 * ch - 3, (0, ch))
    across = (device(z, 1 - plane, core), seg)

    def cross(i, ch):
        return remote(
            white_send.at[i, span(ch)],
            white_recv.at[i, span(ch)],
            wh_ss.at[0],
            wh_rs.at[ch],
            across,
        )

    for i in range(2):

        def store_own(k, at, value, i=i):
            white_send[i, k, :, at] = value
            white[plane, k, 16 * i : 16 * i + 16, at] = value.astype(F32)

        all_own(i).wait_recv()
        transform(own_recv.at[i], own_gates[i], store_own)
        for pair in [(0, ch) for ch in range(3)] if i == 0 else rest:
            cross(*pair).start()

    acc[...] = jnp.zeros_like(acc)
    prod_b[...] = jnp.zeros_like(prod_b)

    def stack(k, half, prod):
        for l in range(2):
            re_at, im_at = l * 128, 256 + l * 128
            ar, ap, am = [], [], []
            for oo in range(2):
                for h in range(2):
                    slot_at = 2 * (2 * half + oo) + h
                    re = gathered[slot_at, k, :, re_at : re_at + 128].astype(F32)
                    im = gathered[slot_at, k, :, im_at : im_at + 128].astype(F32)
                    for part in (slice(0, 8), slice(8, 16)):
                        ar.append(re[part])
                        ap.append(re[part] + im[part])
                        am.append(re[part] - im[part])
            for c in range(0, 16, 2):
                rows = [[[], [], []], [[], [], []]]
                for cc in (c, c + 1):
                    sums = [[None] * 3, [None] * 3]
                    for g in range(4):
                        at = 8 * g + cc % 8
                        br = white[cc // 8, k, at : at + 1, re_at : re_at + 128]
                        bi = white[cc // 8, k, at : at + 1, im_at : im_at + 128]
                        bs = br + bi
                        for oo in range(2):
                            n = 4 * oo + g
                            sums[oo] = [
                                plus(sums[oo][0], ar[n] * bs),
                                plus(sums[oo][1], ap[n] * br),
                                plus(sums[oo][2], am[n] * bi),
                            ]
                    for oo in range(2):
                        for m in range(3):
                            rows[oo][m].append(sums[oo][m])
                for oo in range(2):
                    at = 256 * half + 128 * oo + 8 * c
                    for m in range(3):
                        lane = 256 * m + 128 * l
                        prod[at : at + 16, lane : lane + 128] = jnp.concatenate(
                            rows[oo][m], 0
                        ).astype(BF16)

    def relay(ch):
        arrive(ch, 0, zs - 1)
        for d in range(1, zs):
            forward(ch, d).start()

    def ready(ch):
        arrive(ch, 1, zs)
        ref = white_recv.at[:, span(ch)]
        remote(ref, ref, wh_ss.at[0], wh_rs.at[ch], partner).wait_recv()
        for i in range(2):
            for j in range(per):
                k = ch * per + j
                white[1 - plane, k, 16 * i : 16 * i + 16, :] = white_recv[i, k].astype(F32)

    bufs = [prod_a, prod_b]

    def chunk(ch, carry):
        relay(ch + 1)
        ready(ch)
        for j in range(per):
            k = ch * per + j
            acc[...] += dot(bufs[1 - j % 2][...], lag_table[jnp.maximum(k - 1, 0)])
            stack(k, 0, bufs[j % 2])
            stack(k, 1, bufs[j % 2])
        return carry

    relay(0)
    lax.fori_loop(0, CHUNKS - 1, chunk, 0)

    def partial(o, p):
        rows = part_send.at[128 * o + 64 * p : 128 * o + 64 * p + 64]
        to = (device(z, p, core), octet_of(o, plane))
        return remote(rows, part_recv.at[seg], rs_ss.at[o, p], rs_rs.at[seg], to)

    def remains(o, p):
        return jnp.logical_and(plane == p, seg == octet_of(o, plane))

    def scatter(half):
        part_send[256 * half : 256 * half + 256] = acc[256 * half : 256 * half + 256].astype(BF16)
        for o in (2 * half, 2 * half + 1):
            for p in range(2):

                @pl.when(jnp.logical_not(remains(o, p)))
                def _(o=o, p=p):
                    partial(o, p).start()

                @pl.when(remains(o, p))
                def _(o=o, p=p):
                    part_recv[pl.ds(seg, 1)] = part_send[
                        128 * o + 64 * p : 128 * o + 64 * p + 64
                    ][None]

    ready(CHUNKS - 1)
    last = chans - per

    def lags(half, k, prod):
        at = slice(256 * half, 256 * half + 256)
        acc[at] += dot(prod[at, :], lag_table[k])

    stack(last, 0, prod_a)
    for half in range(2):
        lags(half, last - 1, prod_b)
    stack(last + 1, 0, prod_b)
    lags(0, last, prod_a)
    stack(last, 1, prod_a)
    lags(0, last + 1, prod_b)
    scatter(0)
    stack(last + 1, 1, prod_b)
    lags(1, last, prod_a)
    lags(1, last + 1, prod_b)
    scatter(1)

    all_sources().wait_send()
    for i in range(2):
        all_own(i).wait_send()
    for n, blocks in enumerate((zs, zs - 1)):
        ref = gathered.at[pl.ds(0, blocks)]
        remote(ref, ref, ag_ss.at[n], ag_rs.at[0, 0], partner).wait_send()
    remote(white_send, white_recv, wh_ss.at[0], wh_rs.at[0], partner).wait_send()

    def landed(d):
        at = lax.rem(seg + d, segs)
        ref = part_recv.at[at]
        remote(ref, ref, rs_ss.at[0, 0], rs_rs.at[at], partner).wait_recv()

    @pl.when(lax.rem(seg + lax.div(seg, 2), 2) != plane)
    def _():
        landed(0)

    for d in range(1, segs):
        landed(d)
    for c in range(8):
        total = part_recv[0, 8 * c : 8 * c + 8, :].astype(F32)
        for j in range(1, segs):
            total += part_recv[j, 8 * c : 8 * c + 8, :].astype(F32)
        out[:, c, :] = total * scale[:, c : c + 1]

    for o in range(zs):
        for p in range(2):

            @pl.when(jnp.logical_not(remains(o, p)))
            def _(o=o, p=p):
                partial(o, p).wait_send()


def local(tables, traces, sources, validity):
    chans = lax.axis_size("chan")
    segs = lax.axis_size("seg")
    vmem = pl.BlockSpec(memory_space=pltpu.VMEM)
    hbm = pl.BlockSpec(memory_space=pl.ANY)
    dma = pltpu.SemaphoreType.DMA
    turned = traces.transpose(0, 2, 1)
    tables = [jnp.asarray(t) for t in tables]
    return pl.pallas_call(
        body,
        name="correlate",
        out_shape=jax.ShapeDtypeStruct((8, 8, LAGS), F32),
        in_specs=[hbm] * 8,
        out_specs=vmem,
        scratch_shapes=[
            pltpu.SMEM(sources.shape, jnp.int32),
            pltpu.VMEM(turned.shape, F32),
            pltpu.VMEM(validity.shape, jnp.int32),
            *[pltpu.VMEM(t.shape, t.dtype) for t in tables],
            pltpu.VMEM((2, chans, 16, 512), jnp.int16),
            pltpu.VMEM((2, chans // 2, 16, 512), jnp.int16),
            pltpu.VMEM((2, chans, 16, 512), jnp.int16),
            pltpu.VMEM((chans, 16, 512), jnp.int16),
            *[pltpu.VMEM((16 * chans, 512), BF16)] * 4,
            pltpu.VMEM((1024, 512), BF16),
            pltpu.VMEM((1024, 512), BF16),
            pltpu.VMEM((16 * chans, 512), F32),
            pltpu.VMEM((2, chans, 32, 512), F32),
            pltpu.VMEM((2, chans, 16, 512), BF16),
            pltpu.VMEM((2, chans, 16, 512), BF16),
            pltpu.VMEM((8, chans, 16, 512), BF16),
            pltpu.VMEM((chans, 768, LAGS), BF16),
            pltpu.VMEM((512, 768), BF16),
            pltpu.VMEM((512, 768), BF16),
            pltpu.VMEM((512, LAGS), F32),
            pltpu.VMEM((512, LAGS), BF16),
            pltpu.VMEM((segs, 64, LAGS), BF16),
            dma((11,)),
            dma((2,)),
            dma((2,)),
            dma((2,)),
            dma((2,)),
            dma((CHUNKS, 2)),
            dma((1,)),
            dma((CHUNKS,)),
            dma((4, 2)),
            dma((segs,)),
        ],
        compiler_params=pltpu.CompilerParams(
            collective_id=0, has_side_effects=True, vmem_limit_bytes=60 * 1024 * 1024
        ),
    )(sources, turned, validity, *tables)


def solution(mesh):
    chans = mesh.shape["chan"]
    length = 7680
    tables = constant_tables(length, chans)
    return jax.shard_map(
        functools.partial(local, tables),
        mesh=mesh,
        in_specs=(P("seg", None, "chan"), P(), P()),
        out_specs=P("seg", "chan", None),
        check_vma=False,
    )
```

```python
import functools
import math

import jax
import jax.numpy as jnp
import numpy as np
from jax import lax
from jax.experimental import pallas as pl
from jax.experimental.pallas import tpu as pltpu
from jax.sharding import PartitionSpec as P

LAGS = 512
EPSILON = 1e-06
MESH = pl.DeviceIdType.MESH
CHUNKS = 8
STEPS = 32000.0
F32 = jnp.float32
BF16 = jnp.bfloat16


def constant_tables(length, blocks):
    block_len = length // blocks
    half = block_len // 2
    q = np.arange(block_len)[:, None]
    k1 = np.arange(blocks)[:, None]
    k2 = np.arange(half)[None, :]
    angle = 2.0 * math.pi / length * ((k1 * q.T) % length)
    twist = np.zeros((2, blocks, 512), np.float32)
    twist[0, :, :block_len] = np.cos(angle)
    twist[1, :, :block_len] = np.sin(angle)
    angle = 2.0 * math.pi / block_len * ((q * k2) % block_len)
    second = np.zeros((2, 512, 256), np.float32)
    second[0, :block_len, :half] = np.cos(angle)
    second[1, :block_len, :half] = np.sin(angle)
    second_hi = second.astype(jnp.bfloat16)
    second_lo = (second - second_hi.astype(np.float32)).astype(jnp.bfloat16)
    lag = (np.arange(LAGS) - LAGS // 2)[None, :]
    angle = 2.0 * math.pi / length * ((k1 * lag) % length)
    lag_one = np.stack([np.cos(angle), np.sin(angle)]).astype(np.float32)
    angle = 2.0 * math.pi / block_len * ((k2.T * lag) % block_len)
    lag_two = np.zeros((2, 256, LAGS), np.float32)
    lag_two[0, :half] = 2.0 * np.cos(angle)
    lag_two[1, :half] = 2.0 * np.sin(angle)
    return twist, second_hi, second_lo, lag_one, lag_two


def times_root(value, k, n):
    re, im = value
    c, s = math.cos(2.0 * math.pi * k / n), math.sin(2.0 * math.pi * k / n)
    if k == 0:
        return value
    if 4 * k == n:
        return (im, -re)
    if 2 * k == n:
        return (-re, None if im is None else -im)
    if im is None:
        return (re * c, re * (-s))
    return (re * c + im * s, im * c - re * s)


def plus(a, b):
    if a is None:
        return b
    return a if b is None else a + b


def conj(value):
    re, im = value
    return (re, None if im is None else -im)


def real_dft(xs):
    n = len(xs)
    if n == 2:
        return [(xs[0] + xs[1], None), (xs[0] - xs[1], None)]
    even, odd = real_dft(xs[0::2]), real_dft(xs[1::2])
    h = n // 2
    out = []
    for k in range(h + 1):
        i = k % h
        e = even[i] if i <= h // 2 else conj(even[h - i])
        o = odd[i] if i <= h // 2 else conj(odd[h - i])
        t = times_root(o, k, n)
        out.append((plus(e[0], t[0]), plus(e[1], t[1])))
    return out


def split(value):
    hi = value.astype(BF16)
    return hi, (value - hi.astype(F32)).astype(BF16)


def dot(a, b):
    return jnp.dot(a, b, preferred_element_type=F32)


def body(
    sources,
    traces,
    validity,
    twist_in,
    second_hi,
    second_lo,
    lag_one,
    lag_two,
    out,
    names_smem,
    staged,
    valid_in,
    twist,
    sec_hi,
    sec_lo,
    one,
    two,
    own_send,
    src_send,
    own_recv,
    src_recv,
    hi_a,
    hi_b,
    lo_a,
    lo_b,
    table_hi,
    table_lo,
    spec,
    white,
    white_send,
    white_recv,
    gathered,
    lag_table,
    prod_a,
    prod_b,
    acc,
    part_send,
    part_recv,
    in_sem,
    own_ss,
    own_rs,
    src_sem,
    ag_ss,
    ag_rs,
    wh_ss,
    wh_rs,
    rs_ss,
    rs_rs,
):
    chans = lax.axis_size("chan")
    segs = lax.axis_size("seg")
    me = lax.axis_index("chan")
    seg = lax.axis_index("seg")
    chip, core = lax.div(me, 2), lax.rem(me, 2)
    z, plane = lax.div(chip, 2), lax.rem(chip, 2)
    zs = chans // 4
    block_len = traces.shape[1]
    partner = (2 * chip + 1 - core, seg)

    def iota(shape, axis):
        return lax.broadcasted_iota(jnp.int32, shape, axis)

    def remote(src, dst, send, recv, to):
        return pltpu.make_async_remote_copy(
            src_ref=src,
            dst_ref=dst,
            send_sem=send,
            recv_sem=recv,
            device_id=to,
            device_id_type=MESH,
        )

    def device(zz, pp, cc):
        return lax.rem(zz, zs) * 4 + pp * 2 + cc

    def octet_of(zz, pp):
        return 2 * zz + lax.rem(zz + pp, 2)

    barrier = pltpu.get_barrier_semaphore()
    for d in sorted(range(1, chans), key=lambda d: abs(d - chans // 2)):
        pl.semaphore_signal(
            barrier, inc=1, device_id=(lax.rem(me + d, chans), seg), device_id_type=MESH
        )
    for d in range(1, segs):
        for p in range(2):
            pl.semaphore_signal(
                barrier,
                inc=1,
                device_id=(device(z, p, core), lax.rem(seg + d, segs)),
                device_id_type=MESH,
            )

    fetch = [
        pltpu.make_async_copy(a, b, in_sem.at[n])
        for n, (a, b) in enumerate(
            [(traces.at[g], staged.at[g]) for g in range(4)]
            + [
                (sources, names_smem),
                (validity, valid_in),
                (twist_in, twist),
                (second_hi, sec_hi),
                (second_lo, sec_lo),
                (lag_one, one),
                (lag_two, two),
            ]
        )
    ]
    for n in (4, 0, 1, 2, 3, 7, 8, 9, 10, 5, 6):
        fetch[n].start()

    fetch[4].wait()
    all_chans = staged.shape[2]
    count = 8 * chans // 2
    names = jnp.zeros((count, 1), jnp.int32)
    r_names = iota((count, 1), 0)
    for s in range(count):
        names = jnp.where(r_names == s, names_smem[s], names)
    row = iota((all_chans, 1), 0)
    pick = jnp.concatenate([row, names], 0)
    pick = (iota((all_chans + count, all_chans), 1) == pick).astype(F32).astype(BF16)

    def steps_of(g):
        fetch[g].wait()
        x = staged[g]
        top = jnp.maximum(jnp.max(jnp.abs(x), axis=0, keepdims=True), 1e-30)
        power = jnp.ceil(jnp.log(top) * (128.0 / math.log(2.0))) + 1.0
        steps = jnp.round(x * (STEPS / jnp.exp2(power * (1.0 / 128.0))))
        tail = jnp.where(iota((512 - block_len, all_chans), 0) == 0, power, 0.0)
        steps = jnp.concatenate([steps, tail], 0)
        high = jnp.round(steps * (1.0 / 256.0))
        low = steps - 256.0 * high
        dims = (((1,), (1,)), ((), ()))
        return 256.0 * lax.dot_general(
            pick, high.astype(BF16), dims, preferred_element_type=F32
        ) + lax.dot_general(pick, low.astype(BF16), dims, preferred_element_type=F32)

    for i in range(2):
        pair = [steps_of(2 * i + gg).reshape(-1, 8, 512) for gg in range(2)]
        both = jnp.concatenate(pair, axis=1).astype(jnp.int32).astype(jnp.int16)
        own_send[i] = both[:chans]
        src_send[i] = both[chans:]

    pl.semaphore_wait(barrier, chans - 1 + 2 * (segs - 1))

    others = pl.ds(0, chans - 1)
    peers = sorted(
        [(dz, dx, dc) for dz in range(zs) for dx in range(2) for dc in range(2)][1:],
        key=lambda t: -(2 * min(t[0], zs - t[0]) + 4 * t[1] + t[2]),
    )

    def peer(t):
        return device(z + t[0], lax.rem(plane + t[1], 2), lax.rem(core + t[2], 2))

    for t in peers:
        to = peer(t)
        remote(
            src_send.at[lax.rem(to, 2), octet_of(lax.div(to, 4), lax.rem(lax.div(to, 2), 2))],
            src_recv.at[me],
            src_sem.at[0],
            src_sem.at[1],
            (to, seg),
        ).start()
    for i in range(2):
        for t in peers:
            to = peer(t)
            remote(
                own_send.at[i, to], own_recv.at[i, me], own_ss.at[i], own_rs.at[i], (to, seg)
            ).start()

    def all_sources():
        ref = src_recv.at[others]
        return remote(ref, ref, src_sem.at[0], src_sem.at[1], partner)

    def all_own(i):
        ref = own_recv.at[i, others]
        return remote(ref, ref, own_ss.at[i], own_rs.at[i], partner)

    src_recv[pl.ds(me, 1)] = src_send[core, pl.ds(octet_of(z, plane), 1)]
    for i in range(2):
        own_recv[i, pl.ds(me, 1)] = own_send[i, pl.ds(me, 1)]

    for n in range(5, 11):
        fetch[n].wait()

    for table, sec in ((table_hi, sec_hi), (table_lo, sec_lo)):
        for n in range(2):
            at, low = slice(256 * n, 256 * n + 256), 512 * n
            table[low : low + 256, :256] = sec[0, at]
            table[low : low + 256, 256:] = -sec[1, at]
            table[low + 256 : low + 512, :256] = sec[1, at]
            table[low + 256 : low + 512, 256:] = sec[0, at]

    def fill(k1, carry):
        c1 = one[0, pl.ds(k1, 1), :]
        s1 = one[1, pl.ds(k1, 1), :]

        def rows(i, inner):
            r = pl.multiple_of(i * 16, 16)
            c2 = two[0, pl.ds(r, 16), :]
            s2 = two[1, pl.ds(r, 16), :]
            c = c1 * c2 - s1 * s2
            s = s1 * c2 + c1 * s2
            lag_table[k1, pl.ds(r, 16), :] = (c - s).astype(BF16)
            lag_table[k1, pl.ds(r + 256, 16), :] = s.astype(BF16)
            lag_table[k1, pl.ds(r + 512, 16), :] = (-c).astype(BF16)
            return inner

        return lax.fori_loop(0, 16, rows, carry)

    lax.fori_loop(0, chans, fill, 0)
    first = iota((16, LAGS), 0) == 0
    for r in (0, 256, 512):
        head = lag_table[0, r : r + 16, :].astype(F32)
        lag_table[0, r : r + 16, :] = jnp.where(first, 0.5 * head, head).astype(BF16)

    valid = valid_in[...].astype(F32).astype(BF16)
    all_segs = valid.shape[0]

    def gate_of(row_seg, row_chan, rows):
        seg_hot = (iota((rows, all_segs), 1) == row_seg).astype(F32).astype(BF16)
        chan_hot = (iota((rows, all_chans), 1) == row_chan).astype(F32)
        return jnp.sum(dot(seg_hot, valid) * chan_hot, axis=1, keepdims=True)

    def named(r, base):
        found = jnp.zeros(r.shape, jnp.int32)
        for s in range(8):
            found = jnp.where(r == s, names_smem[8 * base + s], found)
        return found

    r16 = iota((16, 1), 0)
    own_gates = [
        gate_of(4 * seg + 2 * i + r16 // 8, 8 * me + r16 % 8, 16) for i in range(2)
    ]
    src_gate = gate_of(4 * seg + 2 * core + r16 // 8, named(r16 % 8, octet_of(z, plane)), 16)
    want = iota((8, all_chans), 1) == named(iota((8, 1), 0), seg)
    want_valid = lax.dot_general(
        want.astype(F32).astype(BF16),
        valid,
        (((1,), (1,)), ((), ())),
        preferred_element_type=F32,
    ).astype(BF16)
    pairs_all = dot(want_valid, valid)
    shift_hot = (iota((all_chans, 128), 0) == 8 * me + iota((all_chans, 128), 1)).astype(F32)
    pairs = dot(pairs_all.astype(BF16), shift_hot.astype(BF16))
    bins_total = chans * block_len // 2
    scale = 1.0 / jnp.sqrt(2.0 * bins_total * jnp.maximum(pairs, 1.0))

    spread = (iota((256, 256), 0) // 8 == iota((256, 256), 1) // 8).astype(F32).astype(BF16)

    def half_dot(hi, lo, low):
        at = slice(low, low + 512)
        return (
            dot(hi[...], table_hi[at]) + dot(lo[...], table_hi[at]) + dot(hi[...], table_lo[at])
        )

    def transform(recv, gate, store):
        units = []
        for p in range(chans):
            last = recv[p, :, 384:512].astype(jnp.int32).astype(F32)
            at = block_len - 384
            units.append(jnp.exp2(last[:, at : at + 1] * (1.0 / 128.0)) * (1.0 / STEPS))
        for a in range(0, 512, 128):
            h_hi, h_lo = (hi_a, lo_a) if a < 256 else (hi_b, lo_b)
            xs = [
                recv[p, :, a : a + 128].astype(jnp.int32).astype(F32) * units[p]
                for p in range(chans)
            ]
            half = real_dft(xs)
            for k in range(chans):
                g = half[k] if k <= chans // 2 else conj(half[chans - k])
                re, im = g
                c = twist[0, k : k + 1, a : a + 128]
                s = twist[1, k : k + 1, a : a + 128]
                if im is None:
                    re, im = re * c, -(re * s)
                else:
                    re, im = re * c + im * s, im * c - re * s
                at = slice(16 * k, 16 * k + 16)
                hi, lo = split(re)
                b = a % 256
                h_hi[at, b : b + 128] = hi
                h_lo[at, b : b + 128] = lo
                hi, lo = split(im)
                h_hi[at, 256 + b : 384 + b] = hi
                h_lo[at, 256 + b : 384 + b] = lo
            if a == 128:
                spec[...] = half_dot(hi_a, lo_a, 0)
        spec[...] += half_dot(hi_b, lo_b, 512)
        total = None
        for k in range(chans):
            re, im = spec[16 * k : 16 * k + 16, :256], spec[16 * k : 16 * k + 16, 256:]
            total = plus(total, jnp.sqrt(re * re + im * im))
        hi, lo = split(total)
        mean = (dot(hi, spread) + dot(lo, spread)) * (1.0 / 128.0) + EPSILON
        factor = gate / mean
        for k in range(chans):
            for part in range(2):
                at = slice(256 * part, 256 * part + 256)
                store(k, at, (spec[16 * k : 16 * k + 16, at] * factor).astype(BF16))

    per = chans // CHUNKS
    slot = 2 * z + core

    def span(ch):
        return pl.ds(ch * per, per)

    def store_src(k, at, value):
        gathered[slot, k, :, at] = value

    all_sources().wait_recv()
    transform(src_recv, src_gate, store_src)

    def gather(ch, d):
        ref = gathered.at[slot, span(ch)]
        to = partner if d == 0 else (device(z + d, plane, core), seg)
        return remote(ref, ref, ag_ss.at[0], ag_rs.at[ch, int(d == 0)], to)

    def slot_of(d, cc):
        return 2 * lax.rem(z + d, zs) + cc

    def forward(ch, d):
        at = slot_of(d, core)
        ref = gathered.at[at, span(ch)]
        return remote(ref, ref, ag_ss.at[1], ag_rs.at[ch, 1], partner)

    def arrive(ch, way, blocks):
        ref = gathered.at[pl.ds(0, blocks), span(ch)]
        remote(ref, ref, ag_ss.at[0], ag_rs.at[ch, way], partner).wait_recv()

    for ch in range(CHUNKS):
        for d in range(zs - 1, -1, -1):
            gather(ch, d).start()

    rest = [(1, ch) for ch in range(CHUNKS)]
    for ch in range(2, CHUNKS):
        rest.insert(2 * ch - 2, (0, ch))
    across = (device(z, 1 - plane, core), seg)

    def cross(i, ch):
        return remote(
            white_send.at[i, span(ch)],
            white_recv.at[i, span(ch)],
            wh_ss.at[0],
            wh_rs.at[ch],
            across,
        )

    for i in range(2):

        def store_own(k, at, value, i=i):
            white_send[i, k, :, at] = value
            white[plane, k, 16 * i : 16 * i + 16, at] = value.astype(F32)

        all_own(i).wait_recv()
        transform(own_recv.at[i], own_gates[i], store_own)
        for pair in [(0, ch) for ch in range(2)] if i == 0 else rest:
            cross(*pair).start()

    acc[...] = jnp.zeros_like(acc)
    prod_b[...] = jnp.zeros_like(prod_b)

    def stack(k, half, prod):
        for l in range(2):
            re_at, im_at = l * 128, 256 + l * 128
            ar, ap, am = [], [], []
            for oo in range(2):
                for h in range(2):
                    slot_at = 2 * (2 * half + oo) + h
                    re = gathered[slot_at, k, :, re_at : re_at + 128].astype(F32)
                    im = gathered[slot_at, k, :, im_at : im_at + 128].astype(F32)
                    for part in (slice(0, 8), slice(8, 16)):
                        ar.append(re[part])
                        ap.append(re[part] + im[part])
                        am.append(re[part] - im[part])
            for c in range(0, 16, 2):
                rows = [[[], [], []], [[], [], []]]
                for cc in (c, c + 1):
                    sums = [[None] * 3, [None] * 3]
                    for g in range(4):
                        at = 8 * g + cc % 8
                        br = white[cc // 8, k, at : at + 1, re_at : re_at + 128]
                        bi = white[cc // 8, k, at : at + 1, im_at : im_at + 128]
                        bs = br + bi
                        for oo in range(2):
                            n = 4 * oo + g
                            sums[oo] = [
                                plus(sums[oo][0], ar[n] * bs),
                                plus(sums[oo][1], ap[n] * br),
                                plus(sums[oo][2], am[n] * bi),
                            ]
                    for oo in range(2):
                        for m in range(3):
                            rows[oo][m].append(sums[oo][m])
                for oo in range(2):
                    at = 256 * half + 128 * oo + 8 * c
                    for m in range(3):
                        lane = 256 * m + 128 * l
                        prod[at : at + 16, lane : lane + 128] = jnp.concatenate(
                            rows[oo][m], 0
                        ).astype(BF16)

    def relay(ch):
        arrive(ch, 0, zs - 1)
        for d in range(1, zs):
            forward(ch, d).start()

    def ready(ch):
        arrive(ch, 1, zs)
        ref = white_recv.at[:, span(ch)]
        remote(ref, ref, wh_ss.at[0], wh_rs.at[ch], partner).wait_recv()
        for i in range(2):
            for j in range(per):
                k = ch * per + j
                white[1 - plane, k, 16 * i : 16 * i + 16, :] = white_recv[i, k].astype(F32)

    bufs = [prod_a, prod_b]

    def chunk(ch, carry):
        pl.when(ch + 2 < CHUNKS)(lambda: relay(ch + 2))
        ready(ch)
        for j in range(per):
            k = ch * per + j
            acc[...] += dot(bufs[1 - j % 2][...], lag_table[jnp.maximum(k - 1, 0)])
            stack(k, 0, bufs[j % 2])
            stack(k, 1, bufs[j % 2])
        return carry

    relay(0)
    relay(1)
    lax.fori_loop(0, CHUNKS - 1, chunk, 0)

    def partial(o, p):
        rows = part_send.at[128 * o + 64 * p : 128 * o + 64 * p + 64]
        to = (device(z, p, core), octet_of(o, plane))
        return remote(rows, part_recv.at[seg], rs_ss.at[o, p], rs_rs.at[seg], to)

    def remains(o, p):
        return jnp.logical_and(plane == p, seg == octet_of(o, plane))

    def scatter(half):
        part_send[256 * half : 256 * half + 256] = acc[256 * half : 256 * half + 256].astype(BF16)
        for o in (2 * half, 2 * half + 1):
            for p in range(2):

                @pl.when(jnp.logical_not(remains(o, p)))
                def _(o=o, p=p):
                    partial(o, p).start()

                @pl.when(remains(o, p))
                def _(o=o, p=p):
                    part_recv[pl.ds(seg, 1)] = part_send[
                        128 * o + 64 * p : 128 * o + 64 * p + 64
                    ][None]

    ready(CHUNKS - 1)
    last = chans - per

    def lags(half, k, prod):
        at = slice(256 * half, 256 * half + 256)
        acc[at] += dot(prod[at, :], lag_table[k])

    stack(last, 0, prod_a)
    for half in range(2):
        lags(half, last - 1, prod_b)
    stack(last + 1, 0, prod_b)
    lags(0, last, prod_a)
    stack(last, 1, prod_a)
    lags(0, last + 1, prod_b)
    scatter(0)
    stack(last + 1, 1, prod_b)
    lags(1, last, prod_a)
    lags(1, last + 1, prod_b)
    scatter(1)

    all_sources().wait_send()
    for i in range(2):
        all_own(i).wait_send()
    for n, blocks in enumerate((zs, zs - 1)):
        ref = gathered.at[pl.ds(0, blocks)]
        remote(ref, ref, ag_ss.at[n], ag_rs.at[0, 0], partner).wait_send()
    remote(white_send, white_recv, wh_ss.at[0], wh_rs.at[0], partner).wait_send()

    def landed(d):
        at = lax.rem(seg + d, segs)
        ref = part_recv.at[at]
        remote(ref, ref, rs_ss.at[0, 0], rs_rs.at[at], partner).wait_recv()

    @pl.when(lax.rem(seg + lax.div(seg, 2), 2) != plane)
    def _():
        landed(0)

    for d in range(1, segs):
        landed(d)
    for c in range(8):
        total = part_recv[0, 8 * c : 8 * c + 8, :].astype(F32)
        for j in range(1, segs):
            total += part_recv[j, 8 * c : 8 * c + 8, :].astype(F32)
        out[:, c, :] = total * scale[:, c : c + 1]

    for o in range(zs):
        for p in range(2):

            @pl.when(jnp.logical_not(remains(o, p)))
            def _(o=o, p=p):
                partial(o, p).wait_send()


def local(tables, traces, sources, validity):
    chans = lax.axis_size("chan")
    segs = lax.axis_size("seg")
    vmem = pl.BlockSpec(memory_space=pltpu.VMEM)
    hbm = pl.BlockSpec(memory_space=pl.ANY)
    dma = pltpu.SemaphoreType.DMA
    turned = traces.transpose(0, 2, 1)
    tables = [jnp.asarray(t) for t in tables]
    return pl.pallas_call(
        body,
        name="correlate",
        out_shape=jax.ShapeDtypeStruct((8, 8, LAGS), F32),
        in_specs=[hbm] * 8,
        out_specs=vmem,
        scratch_shapes=[
            pltpu.SMEM(sources.shape, jnp.int32),
            pltpu.VMEM(turned.shape, F32),
            pltpu.VMEM(validity.shape, jnp.int32),
            *[pltpu.VMEM(t.shape, t.dtype) for t in tables],
            pltpu.VMEM((2, chans, 16, 512), jnp.int16),
            pltpu.VMEM((2, chans // 2, 16, 512), jnp.int16),
            pltpu.VMEM((2, chans, 16, 512), jnp.int16),
            pltpu.VMEM((chans, 16, 512), jnp.int16),
            *[pltpu.VMEM((16 * chans, 512), BF16)] * 4,
            pltpu.VMEM((1024, 512), BF16),
            pltpu.VMEM((1024, 512), BF16),
            pltpu.VMEM((16 * chans, 512), F32),
            pltpu.VMEM((2, chans, 32, 512), F32),
            pltpu.VMEM((2, chans, 16, 512), BF16),
            pltpu.VMEM((2, chans, 16, 512), BF16),
            pltpu.VMEM((8, chans, 16, 512), BF16),
            pltpu.VMEM((chans, 768, LAGS), BF16),
            pltpu.VMEM((512, 768), BF16),
            pltpu.VMEM((512, 768), BF16),
            pltpu.VMEM((512, LAGS), F32),
            pltpu.VMEM((512, LAGS), BF16),
            pltpu.VMEM((segs, 64, LAGS), BF16),
            dma((11,)),
            dma((2,)),
            dma((2,)),
            dma((2,)),
            dma((2,)),
            dma((CHUNKS, 2)),
            dma((1,)),
            dma((CHUNKS,)),
            dma((4, 2)),
            dma((segs,)),
        ],
        compiler_params=pltpu.CompilerParams(
            collective_id=0, has_side_effects=True, vmem_limit_bytes=60 * 1024 * 1024
        ),
    )(sources, turned, validity, *tables)


def solution(mesh):
    chans = mesh.shape["chan"]
    length = 7680
    tables = constant_tables(length, chans)
    return jax.shard_map(
        functools.partial(local, tables),
        mesh=mesh,
        in_specs=(P("seg", None, "chan"), P(), P()),
        out_specs=P("seg", "chan", None),
        check_vma=False,
    )
```

```python
import functools
import math

import jax
import jax.numpy as jnp
import numpy as np
from jax import lax
from jax.experimental import pallas as pl
from jax.experimental.pallas import tpu as pltpu
from jax.sharding import PartitionSpec as P

LAGS = 512
EPSILON = 1e-06
MESH = pl.DeviceIdType.MESH
CHUNKS = 8
STEPS = 32000.0
F32 = jnp.float32
BF16 = jnp.bfloat16


def constant_tables(length, blocks):
    block_len = length // blocks
    half = block_len // 2
    q = np.arange(block_len)[:, None]
    k1 = np.arange(blocks)[:, None]
    k2 = np.arange(half)[None, :]
    angle = 2.0 * math.pi / length * ((k1 * q.T) % length)
    twist = np.zeros((2, blocks, 512), np.float32)
    twist[0, :, :block_len] = np.cos(angle)
    twist[1, :, :block_len] = np.sin(angle)
    angle = 2.0 * math.pi / block_len * ((q * k2) % block_len)
    second = np.zeros((2, 512, 256), np.float32)
    second[0, :block_len, :half] = np.cos(angle)
    second[1, :block_len, :half] = np.sin(angle)
    second_hi = second.astype(jnp.bfloat16)
    second_lo = (second - second_hi.astype(np.float32)).astype(jnp.bfloat16)
    lag = (np.arange(LAGS) - LAGS // 2)[None, :]
    angle = 2.0 * math.pi / length * ((k1 * lag) % length)
    lag_one = np.stack([np.cos(angle), np.sin(angle)]).astype(np.float32)
    angle = 2.0 * math.pi / block_len * ((k2.T * lag) % block_len)
    lag_two = np.zeros((2, 256, LAGS), np.float32)
    lag_two[0, :half] = 2.0 * np.cos(angle)
    lag_two[1, :half] = 2.0 * np.sin(angle)
    return twist, second_hi, second_lo, lag_one, lag_two


def times_root(value, k, n):
    re, im = value
    c, s = math.cos(2.0 * math.pi * k / n), math.sin(2.0 * math.pi * k / n)
    if k == 0:
        return value
    if 4 * k == n:
        return (im, -re)
    if 2 * k == n:
        return (-re, None if im is None else -im)
    if im is None:
        return (re * c, re * (-s))
    return (re * c + im * s, im * c - re * s)


def plus(a, b):
    if a is None:
        return b
    return a if b is None else a + b


def conj(value):
    re, im = value
    return (re, None if im is None else -im)


def real_dft(xs):
    n = len(xs)
    if n == 2:
        return [(xs[0] + xs[1], None), (xs[0] - xs[1], None)]
    even, odd = real_dft(xs[0::2]), real_dft(xs[1::2])
    h = n // 2
    out = []
    for k in range(h + 1):
        i = k % h
        e = even[i] if i <= h // 2 else conj(even[h - i])
        o = odd[i] if i <= h // 2 else conj(odd[h - i])
        t = times_root(o, k, n)
        out.append((plus(e[0], t[0]), plus(e[1], t[1])))
    return out


def split(value):
    hi = value.astype(BF16)
    return hi, (value - hi.astype(F32)).astype(BF16)


def dot(a, b):
    return jnp.dot(a, b, preferred_element_type=F32)


def body(
    sources,
    traces,
    validity,
    twist_in,
    second_hi,
    second_lo,
    lag_one,
    lag_two,
    out,
    names_smem,
    staged,
    valid_in,
    twist,
    sec_hi,
    sec_lo,
    one,
    two,
    own_send,
    src_send,
    own_recv,
    src_recv,
    hi_a,
    hi_b,
    lo_a,
    lo_b,
    table_hi,
    table_lo,
    spec,
    white,
    white_send,
    white_recv,
    gathered,
    lag_table,
    prod_a,
    prod_b,
    acc,
    part_send,
    part_recv,
    in_sem,
    own_ss,
    own_rs,
    src_sem,
    ag_ss,
    ag_rs,
    wh_ss,
    wh_rs,
    rs_ss,
    rs_rs,
):
    chans = lax.axis_size("chan")
    segs = lax.axis_size("seg")
    me = lax.axis_index("chan")
    seg = lax.axis_index("seg")
    chip, core = lax.div(me, 2), lax.rem(me, 2)
    z, plane = lax.div(chip, 2), lax.rem(chip, 2)
    zs = chans // 4
    block_len = traces.shape[1]
    partner = (2 * chip + 1 - core, seg)

    def iota(shape, axis):
        return lax.broadcasted_iota(jnp.int32, shape, axis)

    def remote(src, dst, send, recv, to):
        return pltpu.make_async_remote_copy(
            src_ref=src,
            dst_ref=dst,
            send_sem=send,
            recv_sem=recv,
            device_id=to,
            device_id_type=MESH,
        )

    def device(zz, pp, cc):
        return lax.rem(zz, zs) * 4 + pp * 2 + cc

    def octet_of(zz, pp):
        return 2 * zz + lax.rem(zz + pp, 2)

    barrier = pltpu.get_barrier_semaphore()
    for d in sorted(range(1, chans), key=lambda d: abs(d - chans // 2)):
        pl.semaphore_signal(
            barrier, inc=1, device_id=(lax.rem(me + d, chans), seg), device_id_type=MESH
        )
    for d in range(1, segs):
        for p in range(2):
            pl.semaphore_signal(
                barrier,
                inc=1,
                device_id=(device(z, p, core), lax.rem(seg + d, segs)),
                device_id_type=MESH,
            )

    fetch = [
        pltpu.make_async_copy(a, b, in_sem.at[n])
        for n, (a, b) in enumerate(
            [(traces.at[g], staged.at[g]) for g in range(4)]
            + [
                (sources, names_smem),
                (validity, valid_in),
                (twist_in, twist),
                (second_hi, sec_hi),
                (second_lo, sec_lo),
                (lag_one, one),
                (lag_two, two),
            ]
        )
    ]
    for n in (4, 0, 1, 2, 3, 7, 8, 9, 10, 5, 6):
        fetch[n].start()

    fetch[4].wait()
    all_chans = staged.shape[2]
    count = 8 * chans // 2
    names = jnp.zeros((count, 1), jnp.int32)
    r_names = iota((count, 1), 0)
    for s in range(count):
        names = jnp.where(r_names == s, names_smem[s], names)
    row = iota((all_chans, 1), 0)
    pick = jnp.concatenate([row, names], 0)
    pick = (iota((all_chans + count, all_chans), 1) == pick).astype(F32).astype(BF16)

    def steps_of(g):
        fetch[g].wait()
        x = staged[g]
        top = jnp.maximum(jnp.max(jnp.abs(x), axis=0, keepdims=True), 1e-30)
        power = jnp.ceil(jnp.log(top) * (128.0 / math.log(2.0))) + 1.0
        steps = jnp.round(x * (STEPS / jnp.exp2(power * (1.0 / 128.0))))
        tail = jnp.where(iota((512 - block_len, all_chans), 0) == 0, power, 0.0)
        steps = jnp.concatenate([steps, tail], 0)
        high = jnp.round(steps * (1.0 / 256.0))
        low = steps - 256.0 * high
        dims = (((1,), (1,)), ((), ()))
        return 256.0 * lax.dot_general(
            pick, high.astype(BF16), dims, preferred_element_type=F32
        ) + lax.dot_general(pick, low.astype(BF16), dims, preferred_element_type=F32)

    for i in range(2):
        pair = [steps_of(2 * i + gg).reshape(-1, 8, 512) for gg in range(2)]
        both = jnp.concatenate(pair, axis=1).astype(jnp.int32).astype(jnp.int16)
        own_send[i] = both[:chans]
        src_send[i] = both[chans:]

    pl.semaphore_wait(barrier, chans - 1 + 2 * (segs - 1))

    others = pl.ds(0, chans - 1)
    peers = sorted(
        [(dz, dx, dc) for dz in range(zs) for dx in range(2) for dc in range(2)][1:],
        key=lambda t: -(2 * min(t[0], zs - t[0]) + 4 * t[1] + t[2]),
    )

    def peer(t):
        return device(z + t[0], lax.rem(plane + t[1], 2), lax.rem(core + t[2], 2))

    for t in peers:
        to = peer(t)
        remote(
            src_send.at[lax.rem(to, 2), octet_of(lax.div(to, 4), lax.rem(lax.div(to, 2), 2))],
            src_recv.at[me],
            src_sem.at[0],
            src_sem.at[1],
            (to, seg),
        ).start()
    for i in range(2):
        for t in peers:
            to = peer(t)
            remote(
                own_send.at[i, to], own_recv.at[i, me], own_ss.at[i], own_rs.at[i], (to, seg)
            ).start()

    def all_sources():
        ref = src_recv.at[others]
        return remote(ref, ref, src_sem.at[0], src_sem.at[1], partner)

    def all_own(i):
        ref = own_recv.at[i, others]
        return remote(ref, ref, own_ss.at[i], own_rs.at[i], partner)

    src_recv[pl.ds(me, 1)] = src_send[core, pl.ds(octet_of(z, plane), 1)]
    for i in range(2):
        own_recv[i, pl.ds(me, 1)] = own_send[i, pl.ds(me, 1)]

    for n in range(5, 11):
        fetch[n].wait()

    for table, sec in ((table_hi, sec_hi), (table_lo, sec_lo)):
        for n in range(2):
            at, low = slice(256 * n, 256 * n + 256), 512 * n
            table[low : low + 256, :256] = sec[0, at]
            table[low : low + 256, 256:] = -sec[1, at]
            table[low + 256 : low + 512, :256] = sec[1, at]
            table[low + 256 : low + 512, 256:] = sec[0, at]

    def fill(k1, carry):
        c1 = one[0, pl.ds(k1, 1), :]
        s1 = one[1, pl.ds(k1, 1), :]

        def rows(i, inner):
            r = pl.multiple_of(i * 16, 16)
            c2 = two[0, pl.ds(r, 16), :]
            s2 = two[1, pl.ds(r, 16), :]
            c = c1 * c2 - s1 * s2
            s = s1 * c2 + c1 * s2
            lag_table[k1, pl.ds(r, 16), :] = (c - s).astype(BF16)
            lag_table[k1, pl.ds(r + 256, 16), :] = s.astype(BF16)
            lag_table[k1, pl.ds(r + 512, 16), :] = (-c).astype(BF16)
            return inner

        return lax.fori_loop(0, 16, rows, carry)

    lax.fori_loop(0, chans, fill, 0)
    first = iota((16, LAGS), 0) == 0
    for r in (0, 256, 512):
        head = lag_table[0, r : r + 16, :].astype(F32)
        lag_table[0, r : r + 16, :] = jnp.where(first, 0.5 * head, head).astype(BF16)

    valid = valid_in[...].astype(F32).astype(BF16)
    all_segs = valid.shape[0]

    def gate_of(row_seg, row_chan, rows):
        seg_hot = (iota((rows, all_segs), 1) == row_seg).astype(F32).astype(BF16)
        chan_hot = (iota((rows, all_chans), 1) == row_chan).astype(F32)
        return jnp.sum(dot(seg_hot, valid) * chan_hot, axis=1, keepdims=True)

    def named(r, base):
        found = jnp.zeros(r.shape, jnp.int32)
        for s in range(8):
            found = jnp.where(r == s, names_smem[8 * base + s], found)
        return found

    r16 = iota((16, 1), 0)
    own_gates = [
        gate_of(4 * seg + 2 * i + r16 // 8, 8 * me + r16 % 8, 16) for i in range(2)
    ]
    src_gate = gate_of(4 * seg + 2 * core + r16 // 8, named(r16 % 8, octet_of(z, plane)), 16)
    want = iota((8, all_chans), 1) == named(iota((8, 1), 0), seg)
    want_valid = lax.dot_general(
        want.astype(F32).astype(BF16),
        valid,
        (((1,), (1,)), ((), ())),
        preferred_element_type=F32,
    ).astype(BF16)
    pairs_all = dot(want_valid, valid)
    shift_hot = (iota((all_chans, 128), 0) == 8 * me + iota((all_chans, 128), 1)).astype(F32)
    pairs = dot(pairs_all.astype(BF16), shift_hot.astype(BF16))
    bins_total = chans * block_len // 2
    scale = 1.0 / jnp.sqrt(2.0 * bins_total * jnp.maximum(pairs, 1.0))

    spread = (iota((256, 256), 0) // 8 == iota((256, 256), 1) // 8).astype(F32).astype(BF16)

    def half_dot(hi, lo, low):
        at = slice(low, low + 512)
        return (
            dot(hi[...], table_hi[at]) + dot(lo[...], table_hi[at]) + dot(hi[...], table_lo[at])
        )

    def transform(recv, gate, store):
        units = []
        for p in range(chans):
            last = recv[p, :, 384:512].astype(jnp.int32).astype(F32)
            at = block_len - 384
            units.append(jnp.exp2(last[:, at : at + 1] * (1.0 / 128.0)) * (1.0 / STEPS))
        for a in range(0, 512, 128):
            h_hi, h_lo = (hi_a, lo_a) if a < 256 else (hi_b, lo_b)
            xs = [
                recv[p, :, a : a + 128].astype(jnp.int32).astype(F32) * units[p]
                for p in range(chans)
            ]
            half = real_dft(xs)
            for k in range(chans):
                g = half[k] if k <= chans // 2 else conj(half[chans - k])
                re, im = g
                c = twist[0, k : k + 1, a : a + 128]
                s = twist[1, k : k + 1, a : a + 128]
                if im is None:
                    re, im = re * c, -(re * s)
                else:
                    re, im = re * c + im * s, im * c - re * s
                at = slice(16 * k, 16 * k + 16)
                hi, lo = split(re)
                b = a % 256
                h_hi[at, b : b + 128] = hi
                h_lo[at, b : b + 128] = lo
                hi, lo = split(im)
                h_hi[at, 256 + b : 384 + b] = hi
                h_lo[at, 256 + b : 384 + b] = lo
            if a == 128:
                spec[...] = half_dot(hi_a, lo_a, 0)
        spec[...] += half_dot(hi_b, lo_b, 512)
        total = None
        for k in range(chans):
            re, im = spec[16 * k : 16 * k + 16, :256], spec[16 * k : 16 * k + 16, 256:]
            total = plus(total, jnp.sqrt(re * re + im * im))
        hi, lo = split(total)
        mean = (dot(hi, spread) + dot(lo, spread)) * (1.0 / 128.0) + EPSILON
        factor = gate / mean
        for k in range(chans):
            for part in range(2):
                at = slice(256 * part, 256 * part + 256)
                store(k, at, (spec[16 * k : 16 * k + 16, at] * factor).astype(BF16))

    per = chans // CHUNKS
    slot = 2 * z + core

    def span(ch):
        return pl.ds(ch * per, per)

    def store_src(k, at, value):
        gathered[slot, k, :, at] = value

    all_sources().wait_recv()
    transform(src_recv, src_gate, store_src)

    def gather(ch, d):
        ref = gathered.at[slot, span(ch)]
        to = partner if d == 0 else (device(z + d, plane, core), seg)
        return remote(ref, ref, ag_ss.at[0], ag_rs.at[ch, int(d == 0)], to)

    def slot_of(d, cc):
        return 2 * lax.rem(z + d, zs) + cc

    def forward(ch, d):
        at = slot_of(d, core)
        ref = gathered.at[at, span(ch)]
        return remote(ref, ref, ag_ss.at[1], ag_rs.at[ch, 1], partner)

    def arrive(ch, way, blocks):
        ref = gathered.at[pl.ds(0, blocks), span(ch)]
        remote(ref, ref, ag_ss.at[0], ag_rs.at[ch, way], partner).wait_recv()

    for ch in range(CHUNKS):
        for d in range(zs - 1, -1, -1):
            gather(ch, d).start()

    rest = [(1, ch) for ch in range(CHUNKS)]
    for ch in range(2, CHUNKS):
        rest.insert(2 * ch - 2, (0, ch))
    across = (device(z, 1 - plane, core), seg)

    def cross(i, ch):
        return remote(
            white_send.at[i, span(ch)],
            white_recv.at[i, span(ch)],
            wh_ss.at[0],
            wh_rs.at[ch],
            across,
        )

    for i in range(2):

        def store_own(k, at, value, i=i):
            white_send[i, k, :, at] = value
            white[plane, k, 16 * i : 16 * i + 16, at] = value.astype(F32)

        all_own(i).wait_recv()
        transform(own_recv.at[i], own_gates[i], store_own)
        for pair in [(0, ch) for ch in range(2)] if i == 0 else rest:
            cross(*pair).start()

    acc[...] = jnp.zeros_like(acc)
    prod_b[...] = jnp.zeros_like(prod_b)

    def octet_at(pos):
        return lax.rem(lax.div(seg, 2) + (2, 1, 3, 0)[pos], zs)

    def stack(k, half, prod):
        for l in range(2):
            re_at, im_at = l * 128, 256 + l * 128
            ar, ap, am = [], [], []
            for oo in range(2):
                for h in range(2):
                    slot_at = 2 * octet_at(2 * half + oo) + h
                    re = gathered[slot_at, k, :, re_at : re_at + 128].astype(F32)
                    im = gathered[slot_at, k, :, im_at : im_at + 128].astype(F32)
                    for part in (slice(0, 8), slice(8, 16)):
                        ar.append(re[part])
                        ap.append(re[part] + im[part])
                        am.append(re[part] - im[part])
            for c in range(0, 16, 2):
                rows = [[[], [], []], [[], [], []]]
                for cc in (c, c + 1):
                    sums = [[None] * 3, [None] * 3]
                    for g in range(4):
                        at = 8 * g + cc % 8
                        br = white[cc // 8, k, at : at + 1, re_at : re_at + 128]
                        bi = white[cc // 8, k, at : at + 1, im_at : im_at + 128]
                        bs = br + bi
                        for oo in range(2):
                            n = 4 * oo + g
                            sums[oo] = [
                                plus(sums[oo][0], ar[n] * bs),
                                plus(sums[oo][1], ap[n] * br),
                                plus(sums[oo][2], am[n] * bi),
                            ]
                    for oo in range(2):
                        for m in range(3):
                            rows[oo][m].append(sums[oo][m])
                for oo in range(2):
                    at = 256 * half + 128 * oo + 8 * c
                    for m in range(3):
                        lane = 256 * m + 128 * l
                        prod[at : at + 16, lane : lane + 128] = jnp.concatenate(
                            rows[oo][m], 0
                        ).astype(BF16)

    def relay(ch):
        arrive(ch, 0, zs - 1)
        for d in range(1, zs):
            forward(ch, d).start()

    def ready(ch):
        arrive(ch, 1, zs)
        ref = white_recv.at[:, span(ch)]
        remote(ref, ref, wh_ss.at[0], wh_rs.at[ch], partner).wait_recv()
        for i in range(2):
            for j in range(per):
                k = ch * per + j
                white[1 - plane, k, 16 * i : 16 * i + 16, :] = white_recv[i, k].astype(F32)

    bufs = [prod_a, prod_b]

    def chunk(ch, carry):
        pl.when(ch + 2 < CHUNKS)(lambda: relay(ch + 2))
        ready(ch)
        for j in range(per):
            k = ch * per + j
            acc[...] += dot(bufs[1 - j % 2][...], lag_table[jnp.maximum(k - 1, 0)])
            stack(k, 0, bufs[j % 2])
            stack(k, 1, bufs[j % 2])
        return carry

    relay(0)
    relay(1)
    lax.fori_loop(0, CHUNKS - 1, chunk, 0)

    def partial(o, p):
        rows = part_send.at[128 * o + 64 * p : 128 * o + 64 * p + 64]
        to = (device(z, p, core), octet_of(octet_at(o), plane))
        return remote(rows, part_recv.at[seg], rs_ss.at[o, p], rs_rs.at[seg], to)

    def remains(o, p):
        return jnp.logical_and(plane == p, seg == octet_of(octet_at(o), plane))

    def scatter(half):
        part_send[256 * half : 256 * half + 256] = acc[256 * half : 256 * half + 256].astype(BF16)
        for o in (2 * half, 2 * half + 1):
            for p in range(2):

                @pl.when(jnp.logical_not(remains(o, p)))
                def _(o=o, p=p):
                    partial(o, p).start()

                @pl.when(remains(o, p))
                def _(o=o, p=p):
                    part_recv[pl.ds(seg, 1)] = part_send[
                        128 * o + 64 * p : 128 * o + 64 * p + 64
                    ][None]

    ready(CHUNKS - 1)
    last = chans - per

    def lags(half, k, prod):
        at = slice(256 * half, 256 * half + 256)
        acc[at] += dot(prod[at, :], lag_table[k])

    stack(last, 0, prod_a)
    for half in range(2):
        lags(half, last - 1, prod_b)
    stack(last + 1, 0, prod_b)
    lags(0, last, prod_a)
    stack(last, 1, prod_a)
    lags(0, last + 1, prod_b)
    scatter(0)
    stack(last + 1, 1, prod_b)
    lags(1, last, prod_a)
    lags(1, last + 1, prod_b)
    scatter(1)

    all_sources().wait_send()
    for i in range(2):
        all_own(i).wait_send()
    for n, blocks in enumerate((zs, zs - 1)):
        ref = gathered.at[pl.ds(0, blocks)]
        remote(ref, ref, ag_ss.at[n], ag_rs.at[0, 0], partner).wait_send()
    remote(white_send, white_recv, wh_ss.at[0], wh_rs.at[0], partner).wait_send()

    def landed(d):
        at = lax.rem(seg + d, segs)
        ref = part_recv.at[at]
        remote(ref, ref, rs_ss.at[0, 0], rs_rs.at[at], partner).wait_recv()

    @pl.when(lax.rem(seg + lax.div(seg, 2), 2) != plane)
    def _():
        landed(0)

    for d in range(1, segs):
        landed(d)
    for c in range(8):
        total = part_recv[0, 8 * c : 8 * c + 8, :].astype(F32)
        for j in range(1, segs):
            total += part_recv[j, 8 * c : 8 * c + 8, :].astype(F32)
        out[:, c, :] = total * scale[:, c : c + 1]

    for o in range(zs):
        for p in range(2):

            @pl.when(jnp.logical_not(remains(o, p)))
            def _(o=o, p=p):
                partial(o, p).wait_send()


def local(tables, traces, sources, validity):
    chans = lax.axis_size("chan")
    segs = lax.axis_size("seg")
    vmem = pl.BlockSpec(memory_space=pltpu.VMEM)
    hbm = pl.BlockSpec(memory_space=pl.ANY)
    dma = pltpu.SemaphoreType.DMA
    turned = traces.transpose(0, 2, 1)
    tables = [jnp.asarray(t) for t in tables]
    return pl.pallas_call(
        body,
        name="correlate",
        out_shape=jax.ShapeDtypeStruct((8, 8, LAGS), F32),
        in_specs=[hbm] * 8,
        out_specs=vmem,
        scratch_shapes=[
            pltpu.SMEM(sources.shape, jnp.int32),
            pltpu.VMEM(turned.shape, F32),
            pltpu.VMEM(validity.shape, jnp.int32),
            *[pltpu.VMEM(t.shape, t.dtype) for t in tables],
            pltpu.VMEM((2, chans, 16, 512), jnp.int16),
            pltpu.VMEM((2, chans // 2, 16, 512), jnp.int16),
            pltpu.VMEM((2, chans, 16, 512), jnp.int16),
            pltpu.VMEM((chans, 16, 512), jnp.int16),
            *[pltpu.VMEM((16 * chans, 512), BF16)] * 4,
            pltpu.VMEM((1024, 512), BF16),
            pltpu.VMEM((1024, 512), BF16),
            pltpu.VMEM((16 * chans, 512), F32),
            pltpu.VMEM((2, chans, 32, 512), F32),
            pltpu.VMEM((2, chans, 16, 512), BF16),
            pltpu.VMEM((2, chans, 16, 512), BF16),
            pltpu.VMEM((8, chans, 16, 512), BF16),
            pltpu.VMEM((chans, 768, LAGS), BF16),
            pltpu.VMEM((512, 768), BF16),
            pltpu.VMEM((512, 768), BF16),
            pltpu.VMEM((512, LAGS), F32),
            pltpu.VMEM((512, LAGS), BF16),
            pltpu.VMEM((segs, 64, LAGS), BF16),
            dma((11,)),
            dma((2,)),
            dma((2,)),
            dma((2,)),
            dma((2,)),
            dma((CHUNKS, 2)),
            dma((1,)),
            dma((CHUNKS,)),
            dma((4, 2)),
            dma((segs,)),
        ],
        compiler_params=pltpu.CompilerParams(
            collective_id=0, has_side_effects=True, vmem_limit_bytes=60 * 1024 * 1024
        ),
    )(sources, turned, validity, *tables)


def solution(mesh):
    chans = mesh.shape["chan"]
    length = 7680
    tables = constant_tables(length, chans)
    return jax.shard_map(
        functools.partial(local, tables),
        mesh=mesh,
        in_specs=(P("seg", None, "chan"), P(), P()),
        out_specs=P("seg", "chan", None),
        check_vma=False,
    )
```
